256 devices in a mesh: theta: 4 (over x), state: 64 (over z, y, core).
Axes of the slice: x: 4, y: 4, z: 8, core: 2. Of those that a mesh axis runs over, the one named last changes fastest.
Arguments:
- states: bfloat16 [32, 32768, 256], P('theta', 'state'), may hold values from -4.875 to 4.875
- log_vol: bfloat16 [32, 32768], P('theta', 'state'), may hold values from -3 to 3
- transition: bfloat16 [32, 256, 256], P('theta'), may hold values from -0.375 to 0.375
- loading: bfloat16 [256, 128], replicated, may hold values from -0.375 to 0.375
- yields: float32 [3, 128], replicated, may hold values from -5 to 5
- state_noise: bfloat16 [3, 32768, 256], P(None, 'state'), may hold values from -5 to 5
- vol_noise: float32 [3, 32768], P(None, 'state'), may hold values from -5 to 5
- vol_mean: float32 [32], replicated, may hold values from -1.5 to 0
- vol_persist: float32 [32], replicated, may hold values from 0.3 to 0.95
- vol_scale: float32 [32], replicated, may hold values from 0.1 to 0.6
- obs_prec: float32 [32], replicated, may hold values from 0.05 to 4
- prior_loglik: float32 [32], replicated, may hold values from -12 to 12
- ancestors: int32 [32], replicated, may hold values from 0 to 31, as said below
- counts: int32 [3, 32, 64], P(None, 'theta', 'state'), may hold values from 256 to 768, as said below
- local_anc: int32 [3, 32, 49152], P(None, 'theta', 'state'), may hold values from 0 to 511
Outputs:
- final_states: bfloat16 [32, 32768, 256], P('theta', 'state')
- final_vol: bfloat16 [32, 32768], P('theta', 'state')
- loglik: float32 [32], P('theta')
The draws below stay inside these ranges and needn't reach their ends.
Inputs may be any that keep to these rules, and one draw needn't show every extreme that they name: ancestors[i] lies in the group of 8 consecutive indices that holds i or in one of the two groups beside it; at most 4 indices of one group name the group below it and at most 4 name the group above it; both bounds are reached. For each step and parameter particle the counts over the shards sum to 32768; the sum of the counts of shards 0 to j - 1 differs from j * 512 by at most 128, and for each step and particle some shard reaches + 128 and some - 128. `local_anc`: only the first counts[t, i, j] slots of shard j's block are used.
All inputs are finite; a program needn't handle non-finite values.
Results may differ from the reference program's by a relative error of at most 0.001.
The reference program's roundings to bfloat16 on the way (of `cloud`) count: a program that leaves them out, or rounds other values in their place, can miss the bound.
Values may be sent and summed in bfloat16 or wider, within the bound.
A program may use at most 64 MiB of HBM per device.

```python
import math
import jax
import jax.numpy as jnp
from jax import lax

K = 256
M = 128
P_DEV = 8
S_DEV = 512
STEPS = 3
MARGIN = 128
P_SIZE = 32
S = 32768
SLOTS = 49152


def draw_states(key, part):
    slot = jnp.arange(S, dtype=jnp.float32)
    scale = 0.6 + 0.6 * slot / S
    base = jnp.clip(jax.random.normal(key, (P_SIZE, S, K), jnp.float32), -4.0, 4.0)
    return (base * scale[None, :, None]).astype(jnp.bfloat16)


def draw_obs_prec(key, part):
    low, high = (0.05, 0.2)
    unit = jax.random.uniform(key, (P_SIZE,), jnp.float32)
    return jnp.exp(jnp.log(low) + unit * (jnp.log(high) - jnp.log(low)))


def draw_ancestors(key, part):
    keys = jax.random.split(jax.random.fold_in(key, 11), 4)
    groups = P_SIZE // P_DEV
    half = P_DEV // 2
    index = jnp.arange(P_SIZE, dtype=jnp.int32)
    group = index // P_DEV
    scores = jax.random.randint(keys[0], (P_SIZE,), 0, 1 << 20) * P_SIZE + index
    ranks = jnp.argsort(jnp.argsort(scores.reshape(groups, P_DEV), axis=1), axis=1).reshape(P_SIZE)
    coin = jax.random.randint(keys[1], (P_SIZE,), 0, 2) == 1
    chosen = jax.random.randint(keys[2], (), 1, groups - 1)
    moving = coin | (group == chosen)
    offset = jnp.where(moving, jnp.where(ranks < half, -1, 1), 0)
    offset = jnp.where((group == 0) & (offset == -1), 0, offset)
    offset = jnp.where((group == groups - 1) & (offset == 1), 0, offset)
    local = jax.random.randint(keys[3], (P_SIZE,), 0, P_DEV)
    return ((group + offset) * P_DEV + local).astype(jnp.int32)


def draw_counts(key, part):
    keys = jax.random.split(jax.random.fold_in(key, 23), 2)
    shards = S // S_DEV
    margin = S_DEV // 4
    inner = jax.random.randint(keys[0], (STEPS, P_SIZE, shards - 1), -margin, margin + 1)
    first = jax.random.randint(keys[1], (STEPS, P_SIZE, 1), 0, shards - 1)
    second = (first + 1) % (shards - 1)
    place = jnp.arange(shards - 1, dtype=jnp.int32)[None, None, :]
    inner = jnp.where(place == first, margin, inner)
    inner = jnp.where(place == second, -margin, inner)
    zeros = jnp.zeros((STEPS, P_SIZE, 1), jnp.int32)
    excess = jnp.concatenate([zeros, inner.astype(jnp.int32), zeros], axis=2)
    return (S_DEV + excess[:, :, 1:] - excess[:, :, :-1]).astype(jnp.int32)


def with_ends(drawn, rng, smallest, high):
    spot = [jax.random.randint(jax.random.fold_in(rng, axis), (), 0, length) for axis, length in enumerate(drawn.shape)]
    main_axis = drawn.shape.index(max(drawn.shape))
    next_to = spot[:main_axis] + [(spot[main_axis] + 1) % drawn.shape[main_axis]] + spot[main_axis + 1:]
    return drawn.at[tuple(spot)].set(smallest).at[tuple(next_to)].set(high)


def level_of(rng, shape, cuts, least, high):
    factor_of = 1.0
    for axis_at, parts in cuts:
        draws = jax.random.uniform(jax.random.fold_in(jax.random.fold_in(rng, 6), axis_at), (parts,), jnp.float32, least / len(cuts), high / len(cuts))
        factor_of = factor_of * jnp.repeat(jnp.exp(draws), shape[axis_at] // parts).reshape((-1,) + (1,) * (len(shape) - 1 - axis_at))
    return factor_of


def gaussian(rng, extent, scale, most, cuts=(), kind=jnp.bfloat16):
    array = jax.random.normal(rng, extent, jnp.float32) * scale
    if len(cuts) > 0:
        array = level_of(rng, extent, cuts, -0.22, 0.18) * array
    return jnp.clip(array, min=-most, max=most).astype(kind)


def setup_inputs(seed: int = 0) -> dict:
    splits = jax.random.split(jax.random.key(seed), 16)
    return {
        "states": draw_states(jax.random.fold_in(splits[15], 71), 0),
        "log_vol": gaussian(splits[1], (P_SIZE, S), 0.5, 3.0, ((0, 4), (1, 64))),
        "transition": gaussian(splits[2], (P_SIZE, K, K), K ** -0.5, 0.375, ((0, 4),)),
        "loading": gaussian(splits[3], (K, M), K ** -0.5, 0.375),
        "yields": gaussian(splits[4], (STEPS, M), 1.0, 5.0, (), jnp.float32),
        "state_noise": gaussian(splits[5], (STEPS, S, K), 1.0, 5.0, ((1, 64),)),
        "vol_noise": gaussian(splits[6], (STEPS, S), 1.0, 5.0, ((1, 64),), jnp.float32),
        "vol_mean": jnp.clip(jax.random.uniform(splits[7], (P_SIZE,), jnp.float32, -1.5, 0.0), -1.5, 0.0),
        "vol_persist": jnp.clip(jax.random.uniform(splits[8], (P_SIZE,), jnp.float32, 0.3, 0.95), 0.3, 0.95),
        "vol_scale": jnp.clip(jnp.exp(jax.random.uniform(splits[9], (P_SIZE,), jnp.float32, math.log(0.1), math.log(0.6))), 0.1, 0.6),
        "obs_prec": draw_obs_prec(jax.random.fold_in(splits[15], 71), 0),
        "prior_loglik": gaussian(splits[11], (P_SIZE,), 3.0, 12.0, (), jnp.float32),
        "ancestors": draw_ancestors(jax.random.fold_in(splits[15], 71), 0),
        "counts": draw_counts(jax.random.fold_in(splits[15], 71), 0),
        "local_anc": with_ends(jax.random.randint(splits[14], (STEPS, P_SIZE, SLOTS), 0, S_DEV), jax.random.fold_in(splits[14], 1), 0, S_DEV - 1).astype(jnp.int32),
    }


def reference(states, log_vol, transition, loading, yields, state_noise, vol_noise, vol_mean, vol_persist, vol_scale, obs_prec, prior_loglik, ancestors, counts, local_anc):
    shard_slots = S_DEV + 2 * MARGIN
    positions = jnp.arange(S, dtype=jnp.int32)

    def particle(which):
        source = ancestors[which]
        cloud = states[source]
        vols = log_vol[source]
        matrix = transition[source]
        center = vol_mean[source]
        persist = vol_persist[source]
        spread = vol_scale[source]
        precision = obs_prec[source]
        total = prior_loglik[source]
        for step in range(STEPS):
            number = counts[step, which].astype(jnp.int32)
            starts = (jnp.cumsum(number) - number).astype(jnp.int32)
            owner = (jnp.sum((starts[None, :] <= positions[:, None]).astype(jnp.int32), axis=1) - 1).astype(jnp.int32)
            offset = (positions - starts[owner]).astype(jnp.int32)
            chosen = local_anc[step, which][owner * shard_slots + offset]
            anchor = (owner * S_DEV + chosen).astype(jnp.int32)
            cloud = cloud[anchor]
            vols_now = vols[anchor].astype(jnp.float32)
            vols_now = center + persist * (vols_now - center) + spread * vol_noise[step]
            drift = jnp.dot(cloud, matrix, preferred_element_type=jnp.float32)
            cloud = (drift + jnp.exp(0.5 * vols_now)[:, None] * state_noise[step].astype(jnp.float32)).astype(jnp.bfloat16)
            vols = vols_now.astype(jnp.bfloat16)
            predicted = jnp.dot(cloud, loading, preferred_element_type=jnp.float32)
            misfit = yields[step][None, :] - predicted
            weights_log = -0.5 * precision * jnp.sum(misfit * misfit, axis=1) + 0.5 * M * jnp.log(precision)
            peak = jnp.max(weights_log)
            total = total + peak + jnp.log(jnp.sum(jnp.exp(weights_log - peak))) - math.log(S)
        return cloud, vols, total

    return lax.map(particle, jnp.arange(P_SIZE, dtype=jnp.int32))
```

```python
import math

import jax
import jax.numpy as jnp
from jax import lax
from jax.experimental import pallas as pl
from jax.experimental.pallas import tpu as pltpu
from jax.sharding import PartitionSpec as P

K = 256
M = 128
PD = 8
SD = 512
STEPS = 3
MARGIN = 128
FRAME = SD + 2 * MARGIN
EXT = K + 16
KEEP = 4
TN = 4
JN = 64
WN = 8
F32 = jnp.float32
BF16 = jnp.bfloat16
I32 = jnp.int32
MESH = pl.DeviceIdType.MESH


def nt(a, b):
    return lax.dot_general(a, b, (((1,), (1,)), ((), ())), preferred_element_type=F32)


def nn(a, b):
    return lax.dot_general(a, b, (((1,), (0,)), ((), ())), preferred_element_type=F32)


def iota(shape, dim):
    return lax.broadcasted_iota(I32, shape, dim)


def eye(n):
    return jnp.where(iota((n, n), 0) == iota((n, n), 1), 1.0, 0.0).astype(BF16)


def kernel(
    anc, cnt, vm_s, vp_s, vs_s, op_s, pr_s,
    lv, ld, yl, vn, la, states, trans, noise,
    o_states, o_vol, o_ll,
    st, tr, nz, sc, sm, sv, rc, rm, rv,
    cT, own, mT, nT, lT, yb, eL, eR, hL, hR,
    ctile, c2tile, g1, g2, dref, eref, cz, stats, s1, s2, lvf, vf, osb, tmp, eyer,
    perm_s, src_s, rem_s, anc_s, pos_s, snd_s,
    ld_sem, th_ss, th_rs, tv_ss, tv_rs, hl_ss, hl_rs, g_ss, g_rs, out_sem,
):
    g = lax.axis_index("theta")
    j = lax.axis_index("state")
    z, w = j // WN, j % WN
    left, right = (j + JN - 1) % JN, (j + 1) % JN

    def dev(theta, state):
        return {"theta": theta, "state": state}

    barrier = pltpu.get_barrier_semaphore()

    def greet(theta, state):
        pl.semaphore_signal(
            barrier, inc=1, device_id=dev(theta, state), device_id_type=MESH
        )

    for o in range(1, 8):
        greet(g, ((z + o) % 8) * WN + w)
    for o in range(1, WN):
        greet(g, z * WN + (w + o) % WN)
    greet(g, left)
    greet(g, right)

    @pl.when(g > 0)
    def _():
        greet(g - 1, j)

    @pl.when(g < TN - 1)
    def _():
        greet(g + 1, j)

    load_st = pltpu.make_async_copy(states, st, ld_sem.at[0])
    load_tr = pltpu.make_async_copy(trans, tr, ld_sem.at[1])
    load_nz = pltpu.make_async_copy(noise, nz, ld_sem.at[2])
    load_st.start()
    load_tr.start()
    load_nz.start()

    a8 = [anc[g * PD + i] for i in range(PD)]
    off = [lax.shift_right_arithmetic(a, 3) - g for a in a8]
    below = [jnp.where(o == -1, 1, 0) for o in off]
    above = [jnp.where(o == 1, 1, 0) for o in off]
    nb, na, nl = 0, 0, 0
    rank_b, rank_a, rank_l = [], [], []
    for i in range(PD):
        rank_b.append(nb)
        rank_a.append(na)
        rank_l.append(nl)
        nb = nb + below[i]
        na = na + above[i]
        nl = nl + 1 - below[i] - above[i]
    free_b = KEEP - nb
    pos = []
    for i in range(PD):
        l = rank_l[i]
        home = jnp.where(l < free_b, 2 * (nb + l), 2 * (na + l - free_b) + 1)
        slot = jnp.where(
            below[i] == 1,
            2 * rank_b[i],
            jnp.where(above[i] == 1, 2 * rank_a[i] + 1, home),
        )
        pos.append(jnp.clip(slot, 0, PD - 1))
        pos_s[i] = pos[i]
    for n in range(PD):
        who, a = 0, 0
        for i in range(PD):
            hit = pos[i] == n
            who = jnp.where(hit, i, who)
            a = jnp.where(hit, a8[i], a)
        perm_s[n] = who
        anc_s[n] = a
        src_s[n] = a & (PD - 1)
        rem_s[n] = jnp.where(lax.shift_right_arithmetic(a, 3) == g, 0, 1)
    for d, peer in ((0, jnp.minimum(g + 1, TN - 1)), (1, jnp.maximum(g - 1, 0))):
        rank = 0
        chosen = [0] * KEEP
        for i in range(PD):
            a = anc[peer * PD + i]
            hit = jnp.where(lax.shift_right_arithmetic(a, 3) == g, 1, 0)
            for k in range(KEEP):
                take = jnp.where(rank == k, hit, 0)
                chosen[k] = jnp.where(take == 1, a & (PD - 1), chosen[k])
            rank = rank + hit
        for k in range(KEEP):
            snd_s[2 * k + d] = chosen[k]

    row8, lane8 = iota((PD, 128), 0), iota((PD, 128), 1)
    tile = jnp.zeros((PD, 128), I32)
    for t in range(STEPS):
        for p in range(PD):
            tile = jnp.where((row8 == p) & (lane8 == t), cnt[t * PD + p], tile)
    ctile[...] = tile
    lvf[...] = lv[...].astype(F32)
    for d in range(2):
        for k in range(KEEP):
            row = lvf[pl.ds(snd_s[2 * k + d], 1), :]
            sv[d, k : k + 1, :] = row
            sv[d, KEEP + k : KEEP + k + 1, :] = row
    load_st.wait()
    load_tr.wait()

    def fill(n, _):
        s = snd_s[n]
        sc[n] = st[s]
        sm[n] = tr[s]
        return 0

    def send_copy(n):
        peer = jnp.where(n % 2 == 0, g + 1, g - 1)
        c = pltpu.make_async_remote_copy(
            sc.at[n], rc.at[n], th_ss.at[0, n], th_rs.at[0, n],
            device_id=dev(peer, j), device_id_type=MESH,
        )
        m = pltpu.make_async_remote_copy(
            sm.at[n], rm.at[n], th_ss.at[1, n], th_rs.at[1, n],
            device_id=dev(peer, j), device_id_type=MESH,
        )
        return c, m

    def send_vol(d):
        peer = jnp.where(d == 0, g + 1, g - 1)
        return pltpu.make_async_remote_copy(
            sv.at[d], rv.at[d], tv_ss.at[d], tv_rs.at[d],
            device_id=dev(peer, j), device_id_type=MESH,
        )

    def group1(o, src, dst, u):
        return pltpu.make_async_remote_copy(
            src, dst.at[o], g_ss.at[u, o], g_rs.at[u, o],
            device_id=dev(g, z * WN + (w + o) % WN), device_id_type=MESH,
        )

    def group2(o, src, dst, u):
        return pltpu.make_async_remote_copy(
            src, dst.at[o], g_ss.at[u, o], g_rs.at[u, o],
            device_id=dev(g, ((z + o) % 8) * WN + w), device_id_type=MESH,
        )

    lax.fori_loop(0, 2, fill, 0)
    pl.semaphore_wait(
        barrier, 16 + jnp.where(g > 0, 1, 0) + jnp.where(g < TN - 1, 1, 0)
    )
    for o in range(1, WN):
        group1(o, ctile, g1, 0).start()

    def each_dir(fn):
        @pl.when(g < TN - 1)
        def _():
            fn(0)

        @pl.when(g > 0)
        def _():
            fn(1)

    def has_in(n):
        return jnp.where(n % 2 == 0, g > 0, g < TN - 1)

    def has_out(n):
        return jnp.where(n % 2 == 0, g < TN - 1, g > 0)

    each_dir(lambda d: send_vol(d).start())

    def start_pair(n, _):
        @pl.when(has_out(n))
        def _():
            c, m = send_copy(n)
            c.start()
            m.start()

        return 0

    lax.fori_loop(0, 2, start_pair, 0)
    lax.fori_loop(2, 2 * KEEP, fill, 0)
    lax.fori_loop(2, 2 * KEEP, start_pair, 0)

    eyer[...] = eye(K)
    load_nz.wait()
    for t in range(STEPS):
        nT[t] = nt(eyer[...], nz[t]).astype(BF16)
        yb[t] = jnp.transpose(jnp.broadcast_to(yl[t : t + 1, :], (M, M)))
    lT[...] = nt(eye(M), ld[...]).astype(BF16)
    stats[...] = jnp.zeros_like(stats)

    before = jnp.zeros((PD, 128), I32)
    whole = ctile[...]
    for o in range(1, WN):
        group1(o, ctile, g1, 0).wait_recv()
        got = g1[o]
        source = (w + WN - o) % WN
        before = before + jnp.where(source < w, got, 0)
        whole = whole + got
    c2tile[...] = whole
    for o in range(1, 8):
        group2(o, c2tile, g2, 1).start()
    for o in range(1, 8):
        group2(o, c2tile, g2, 1).wait_recv()
        source = (z + 8 - o) % 8
        before = before + jnp.where(source < z, g2[o], 0)
    first = before - SD * j
    for t in range(STEPS):
        d = jnp.broadcast_to(first[:, t : t + 1], (PD, 128))
        e = d + jnp.broadcast_to(tile[:, t : t + 1], (PD, 128))
        dref[t * PD : (t + 1) * PD, :] = d
        eref[t * PD : (t + 1) * PD, :] = e
        shift = jnp.concatenate([d + MARGIN] * (FRAME // 128), axis=1)
        x = la[t * PD : (t + 1) * PD, :]
        for b in range(9):
            x = jnp.where((shift & (1 << b)) != 0, pltpu.roll(x, 1 << b, 1), x)
        cz[t * PD : (t + 1) * PD, :] = x

    def halo(n, t):
        to_left = pltpu.make_async_remote_copy(
            eL.at[n, t], hR.at[n, t], hl_ss.at[0, n, t], hl_rs.at[0, n, t],
            device_id=dev(g, left), device_id_type=MESH,
        )
        to_right = pltpu.make_async_remote_copy(
            eR.at[n, t], hL.at[n, t], hl_ss.at[1, n, t], hl_rs.at[1, n, t],
            device_id=dev(g, right), device_id_type=MESH,
        )
        return to_left, to_right

    def build(n):
        @pl.when(has_in(n))
        def _():
            c, m = send_copy(n)
            c.wait_recv()
            m.wait_recv()

        src = src_s[n]
        remote = rem_s[n] == 1
        eyes = eyer[...]
        cloud = jnp.where(remote, rc[n].astype(F32), st[src].astype(F32)).astype(BF16)
        cT[n, 0:K, :] = nt(eyes, cloud).astype(BF16)
        mat = jnp.where(remote, rm[n].astype(F32), tr[src].astype(F32)).astype(BF16)
        mT[n] = nt(eyes, mat).astype(BF16)
        got = rv[n % 2, pl.ds(n // 2, 1), :]
        vol = jnp.where(remote, got, lvf[pl.ds(src, 1), :])
        cT[n, K:EXT, :] = jnp.broadcast_to(vol, (EXT - K, SD)).astype(BF16)

    def draw(n, t):
        picks = cz[pl.ds(t * PD + perm_s[n], 1), :]
        table = cT[n]
        for b in range(FRAME // 256):
            row = picks[:, b * 256 : (b + 1) * 256]
            hot = jnp.where(iota((SD, 256), 0) == row, 1.0, 0.0).astype(BF16)
            got = nn(table, hot).astype(BF16)
            if b == 0:
                eL[n, t] = got[:, 0:MARGIN]
                own[n, :, 0:128] = got[:, MARGIN:256]
            elif b == 1:
                own[n, :, 128:384] = got
            else:
                own[n, :, 384:512] = got[:, 0:MARGIN]
                eR[n, t] = got[:, MARGIN:256]
        to_left, to_right = halo(n, t)
        to_left.start()
        to_right.start()

    def step(n, t):
        to_left, to_right = halo(n, t)
        to_left.wait_recv()
        to_right.wait_recv()
        at = t * PD + perm_s[n]
        d = dref[pl.ds(at, 1), :]
        e = eref[pl.ds(at, 1), :]
        lane = iota((1, 128), 1)
        a = anc_s[n]
        center, persist, spread, prec = vm_s[a], vp_s[a], vs_s[a], op_s[a]
        front = jnp.where(
            lane < d, hL[n, t].astype(F32), own[n, :, 0:128].astype(F32)
        ).astype(BF16)
        back = jnp.where(
            lane + 384 >= e, hR[n, t].astype(F32), own[n, :, 384:512].astype(F32)
        ).astype(BF16)
        own[n, :, 0:128] = front
        own[n, :, 384:512] = back
        mat = mT[n]
        y = yb[t]
        y = jnp.concatenate([y, y], axis=1)
        weights = []
        for b in range(2):
            cols = slice(b * 256, (b + 1) * 256)
            x = own[n, :, cols]
            vol = x[K:EXT].astype(F32)[0:1]
            h = center + persist * (vol - center) + spread * vn[pl.ds(t, 1), cols]
            drift = nn(mat, x[0:K])
            cloud = (drift + jnp.exp(0.5 * h) * nT[t, :, cols].astype(F32)).astype(BF16)
            hb = h.astype(BF16)
            cT[n, 0:K, cols] = cloud
            cT[n, K:EXT, cols] = jnp.broadcast_to(h, (EXT - K, 256)).astype(BF16)
            vf[pl.ds(n, 1), cols] = hb.astype(F32)
            miss = y - nn(lT[...], cloud)
            ssq = jnp.sum(miss * miss, axis=0, keepdims=True)
            weights.append(-0.5 * prec * ssq)
        logw = jnp.concatenate(weights, axis=1)
        logw = logw + 0.5 * M * jnp.log(jnp.full((1, 1), prec, F32))
        peak = jnp.max(logw, axis=1, keepdims=True)
        mass = jnp.sum(jnp.exp(logw - peak), axis=1, keepdims=True)
        here = lane == t
        stats[pl.ds(n, 1), :] = jnp.where(here, peak, stats[pl.ds(n, 1), :])
        stats[pl.ds(PD + n, 1), :] = jnp.where(here, mass, stats[pl.ds(PD + n, 1), :])

    def both(fn, r, *rest):
        for side in range(2):
            fn(2 * r + side, *rest)

    def wave(r, _):
        @pl.when(r < KEEP)
        def _():
            both(build, r)
            both(draw, r, 0)

        @pl.when(r > 0)
        def _():
            both(step, r - 1, 1)
            both(draw, r - 1, 2)

        @pl.when(r < KEEP)
        def _():
            both(step, r, 0)
            both(draw, r, 1)

        @pl.when(r > 0)
        def _():
            both(step, r - 1, 2)

        return 0

    each_in = ((g > 0, 0), (g < TN - 1, 1))
    for cond, d in each_in:
        @pl.when(cond)
        def _(d=d):
            send_vol(d).wait_recv()

    lax.fori_loop(0, KEEP + 1, wave, 0)

    def join(buf, here):
        order = [buf[(here + 8 - k) % 8] for k in range(8)]
        peak = order[0][0:PD]
        for x in order[1:]:
            peak = jnp.maximum(peak, x[0:PD])
        mass = jnp.zeros((PD, 128), F32)
        for x in order:
            mass = mass + x[PD:] * jnp.exp(x[0:PD] - peak)
        return peak, mass

    s1[0] = stats[...]
    for o in range(1, WN):
        group1(o, stats, s1, 2).start()

    def emit(i, _):
        at = pos_s[i]
        for b in range(2):
            block = cT[at, 0:K, b * 256 : (b + 1) * 256]
            osb[i, b * 256 : (b + 1) * 256, :] = nt(eyer[...], block).astype(BF16)
        pltpu.make_async_copy(osb.at[i], o_states.at[i], out_sem.at[i]).start()
        tmp[pl.ds(i, 1), :] = vf[pl.ds(at, 1), :]
        return 0

    lax.fori_loop(0, PD // 2, emit, 0)
    for o in range(1, WN):
        group1(o, stats, s1, 2).wait_recv()
    peak, mass = join(s1, w)
    s2[0, 0:PD, :] = peak
    s2[0, PD:, :] = mass
    for o in range(1, 8):
        group2(o, s2.at[0], s2, 3).start()
    lax.fori_loop(PD // 2, PD, emit, 0)
    o_vol[...] = tmp[...].astype(BF16)
    for o in range(1, 8):
        group2(o, s2.at[0], s2, 3).wait_recv()
    peak, mass = join(s2, z)
    live = lane8 < STEPS
    part = peak + jnp.log(jnp.where(live, mass, 1.0)) - math.log(SD * JN)
    total = jnp.sum(jnp.where(live, part, 0.0), axis=1, keepdims=True)
    s1[0, 0:PD, :] = jnp.broadcast_to(total, (PD, 128))
    lane1 = iota((1, 128), 1)
    out = jnp.zeros((1, 128), F32)
    for i in range(PD):
        value = s1[0, pl.ds(pos_s[i], 1), :] + pr_s[a8[i]]
        out = jnp.where(lane1 == i, value, out)
    o_ll[...] = out

    for o in range(1, WN):
        group1(o, ctile, g1, 0).wait_send()
        group2(o, c2tile, g2, 1).wait_send()
        group1(o, stats, s1, 2).wait_send()
        group2(o, s2.at[0], s2, 3).wait_send()
    each_dir(lambda d: send_vol(d).wait_send())

    def drain(n, _):
        @pl.when(has_out(n))
        def _():
            c, m = send_copy(n)
            c.wait_send()
            m.wait_send()

        def drain_t(t, _):
            to_left, to_right = halo(n, t)
            to_left.wait_send()
            to_right.wait_send()
            return 0

        lax.fori_loop(0, STEPS, drain_t, 0)
        pltpu.make_async_copy(osb.at[n], o_states.at[n], out_sem.at[n]).wait()
        return 0

    lax.fori_loop(0, PD, drain, 0)


def local(
    states, log_vol, transition, loading, yields, state_noise, vol_noise,
    vol_mean, vol_persist, vol_scale, obs_prec, prior_loglik,
    ancestors, counts, local_anc,
):
    smem = pl.BlockSpec(memory_space=pltpu.SMEM)
    vmem = pl.BlockSpec(memory_space=pltpu.VMEM)
    hbm = pl.BlockSpec(memory_space=pl.ANY)
    dma = pltpu.SemaphoreType.DMA
    v, s = pltpu.VMEM, pltpu.SMEM
    final, vol, ll = pl.pallas_call(
        kernel,
        out_shape=(
            jax.ShapeDtypeStruct((PD, SD, K), BF16),
            jax.ShapeDtypeStruct((PD, SD), BF16),
            jax.ShapeDtypeStruct((1, 128), F32),
        ),
        in_specs=[smem] * 7 + [vmem] * 5 + [hbm] * 3,
        out_specs=(hbm, vmem, vmem),
        scratch_shapes=[
            v((PD, SD, K), BF16), v((PD, K, K), BF16), v((STEPS, SD, K), BF16),
            v((PD, SD, K), BF16), v((PD, K, K), BF16), v((2, PD, SD), F32),
            v((PD, SD, K), BF16), v((PD, K, K), BF16), v((2, PD, SD), F32),
            v((PD, EXT, SD), BF16), v((PD, EXT, SD), BF16), v((PD, K, K), BF16),
            v((STEPS, K, SD), BF16), v((M, K), BF16), v((STEPS, M, M), F32),
            v((PD, STEPS, EXT, MARGIN), BF16), v((PD, STEPS, EXT, MARGIN), BF16),
            v((PD, STEPS, EXT, MARGIN), BF16), v((PD, STEPS, EXT, MARGIN), BF16),
            v((PD, 128), I32), v((PD, 128), I32),
            v((8, PD, 128), I32), v((8, PD, 128), I32),
            v((STEPS * PD, 128), I32), v((STEPS * PD, 128), I32),
            v((STEPS * PD, FRAME), I32),
            v((2 * PD, 128), F32), v((8, 2 * PD, 128), F32), v((8, 2 * PD, 128), F32),
            v((PD, SD), F32), v((PD, SD), F32), v((PD, SD, K), BF16),
            v((PD, SD), F32), v((K, K), BF16),
            s((PD,), I32), s((PD,), I32), s((PD,), I32), s((PD,), I32),
            s((PD,), I32), s((PD,), I32),
            dma((3,)), dma((2, PD)), dma((2, PD)), dma((2,)), dma((2,)),
            dma((2, PD, STEPS)), dma((2, PD, STEPS)),
            dma((4, 8)), dma((4, 8)), dma((PD,)),
        ],
        compiler_params=pltpu.CompilerParams(
            collective_id=0, has_side_effects=True, vmem_limit_bytes=60 << 20
        ),
    )(
        ancestors, counts.reshape(STEPS * PD),
        vol_mean, vol_persist, vol_scale, obs_prec, prior_loglik,
        log_vol, loading, yields, vol_noise, local_anc.reshape(STEPS * PD, FRAME),
        states, transition, state_noise,
    )
    return final, vol, ll[0, :PD]


def solution(mesh):
    placed = (
        P("theta", "state", None),
        P("theta", "state"),
        P("theta", None, None),
        P(),
        P(),
        P(None, "state", None),
        P(None, "state"),
        P(),
        P(),
        P(),
        P(),
        P(),
        P(),
        P(None, "theta", "state"),
        P(None, "theta", "state"),
    )
    return jax.shard_map(
        local,
        mesh=mesh,
        in_specs=placed,
        out_specs=(P("theta", "state", None), P("theta", "state"), P("theta")),
        check_vma=False,
    )
```

```python
import math

import jax
import jax.numpy as jnp
from jax import lax
from jax.experimental import pallas as pl
from jax.experimental.pallas import tpu as pltpu
from jax.sharding import PartitionSpec as P

K = 256
M = 128
PD = 8
SD = 512
STEPS = 3
MARGIN = 128
FRAME = SD + 2 * MARGIN
EXT = K + 16
HALF = K // 2
KEEP = 4
LAST = 2 * KEEP - 2
TN = 4
JN = 64
WN = 8
BUILD, GO, END, SERVE, PASS = range(5)
ORDER = (
    (BUILD, 0, 0), (SERVE, 0, 0), (GO, 0, 0), (BUILD, 1, 0), (PASS, 0, 0),
    (GO, 0, 1), (GO, 1, 0), (BUILD, 2, 0), (END, 0, 2), (GO, 1, 1),
    (GO, 2, 0), (GO, 3, 0), (END, 1, 2), (GO, 2, 1), (GO, 3, 1),
    (END, 2, 2), (END, 3, 2),
)
PACKED = [
    sum((16 * k + 4 * r + t) << (7 * i) for i, (k, r, t) in enumerate(ORDER[at : at + 4]))
    for at in range(0, len(ORDER), 4)
]
F32 = jnp.float32
BF16 = jnp.bfloat16
I32 = jnp.int32
MESH = pl.DeviceIdType.MESH


def nt(a, b):
    return lax.dot_general(a, b, (((1,), (1,)), ((), ())), preferred_element_type=F32)


def nn(a, b):
    return lax.dot_general(a, b, (((1,), (0,)), ((), ())), preferred_element_type=F32)


def iota(shape, dim):
    return lax.broadcasted_iota(I32, shape, dim)


def eye(n):
    return jnp.where(iota((n, n), 0) == iota((n, n), 1), 1.0, 0.0).astype(BF16)


def kernel(
    anc, vm_s, vp_s, vs_s, op_s, pr_s,
    cnt, lv, ld, yl, vn, la, states, trans, noise,
    o_states, o_vol, o_ll, o_pos,
    st, tr, nz, sc, sm, sv, rc, rm, rv, rcT, req, reqin,
    cT, own, mT, nT, lT, yb, eL, eR, hL, hR,
    ctile, c2tile, g1, g2, dref, eref, cz, stats, s1, s2, lvf, osb, eyer, lines,
    perm_s, src_s, rem_s, anc_s, snd_s,
    ld_sem, th_ss, th_rs, rq_ss, rq_rs, fw_ss, fw_rs, tv_ss, tv_rs, hl_ss, hl_rs, g_ss, g_rs, out_sem,
):
    g = lax.axis_index("theta")
    j = lax.axis_index("state")
    z, w, core = j // WN, j % WN, j % 2
    left, right = (j + JN - 1) % JN, (j + 1) % JN

    def dev(theta, state):
        return {"theta": theta, "state": state}

    barrier = pltpu.get_barrier_semaphore()

    def greet(theta, state):
        pl.semaphore_signal(
            barrier, inc=1, device_id=dev(theta, state), device_id_type=MESH
        )

    for o in range(1, 8):
        greet(g, ((z + o) % 8) * WN + w)
    for o in range(1, WN):
        greet(g, z * WN + (w + o) % WN)
    greet(g, left)
    greet(g, right)

    @pl.when(g > 0)
    def _():
        greet(g - 1, j)

    @pl.when(g < TN - 1)
    def _():
        greet(g + 1, j)

    load_st = pltpu.make_async_copy(states, st, ld_sem.at[0])
    load_tr = pltpu.make_async_copy(trans, tr, ld_sem.at[1])
    load_nz = pltpu.make_async_copy(noise, nz, ld_sem.at[2])
    load_st.start()
    load_tr.start()
    load_nz.start()

    a8 = [anc[g * PD + i] for i in range(PD)]
    off = [lax.shift_right_arithmetic(a, 3) - g for a in a8]
    below = [jnp.where(o == -1, 1, 0) for o in off]
    above = [jnp.where(o == 1, 1, 0) for o in off]
    nb, na, nl = 0, 0, 0
    rank_b, rank_a, rank_l = [], [], []
    for i in range(PD):
        rank_b.append(nb)
        rank_a.append(na)
        rank_l.append(nl)
        nb = nb + below[i]
        na = na + above[i]
        nl = nl + 1 - below[i] - above[i]
    free_b = KEEP - nb
    pos = []
    for i in range(PD):
        l = rank_l[i]
        home = jnp.where(l < free_b, 2 * (nb + l), 2 * (na + l - free_b) + 1)
        slot = jnp.where(
            below[i] == 1,
            2 * rank_b[i],
            jnp.where(above[i] == 1, 2 * rank_a[i] + 1, home),
        )
        pos.append(jnp.clip(slot, 0, PD - 1))
        o_pos[i] = pos[i]
    for n in range(PD):
        who, a = 0, 0
        for i in range(PD):
            hit = pos[i] == n
            who = jnp.where(hit, i, who)
            a = jnp.where(hit, a8[i], a)
        perm_s[n] = who
        anc_s[n] = a
        src_s[n] = a & (PD - 1)
        rem_s[n] = jnp.where(lax.shift_right_arithmetic(a, 3) == g, 0, 1)
    for d, peer in ((0, jnp.minimum(g + 1, TN - 1)), (1, jnp.maximum(g - 1, 0))):
        rank = 0
        chosen = [0] * KEEP
        for i in range(PD):
            a = anc[peer * PD + i]
            hit = jnp.where(lax.shift_right_arithmetic(a, 3) == g, 1, 0)
            for k in range(KEEP):
                take = jnp.where(rank == k, hit, 0)
                chosen[k] = jnp.where(take == 1, a & (PD - 1), chosen[k])
            rank = rank + hit
        for k in range(KEEP):
            snd_s[2 * k + d] = chosen[k]

    lane8 = iota((PD, 128), 1)
    tile = jnp.zeros((PD, 128), I32)
    for t in range(STEPS):
        line = jnp.broadcast_to(cnt[t].astype(F32), (PD, PD))
        line = jnp.where(iota((PD, PD), 0) == iota((PD, PD), 1), line, 0.0)
        column = jnp.sum(line, axis=1, keepdims=True).astype(I32)
        tile = jnp.where(lane8 == t, jnp.broadcast_to(column, (PD, 128)), tile)
    ctile[...] = tile
    lvf[...] = lv[...].astype(F32)
    for d in range(2):
        for k in range(KEEP):
            row = lvf[pl.ds(snd_s[2 * k + d], 1), :]
            sv[d, k : k + 1, :] = row
            sv[d, KEEP + k : KEEP + k + 1, :] = row
    load_st.wait()
    load_tr.wait()

    def fill(n, _):
        s = snd_s[n]
        sc[n] = st[s]
        sm[n] = tr[s, pl.ds(pl.multiple_of(core * HALF, HALF), HALF), :]
        return 0

    def send_copy(n):
        peer = jnp.where(n % 2 == 0, g + 1, g - 1)
        return pltpu.make_async_remote_copy(
            sc.at[n], rc.at[n], th_ss.at[0, n], th_rs.at[0, n],
            device_id=dev(peer, j), device_id_type=MESH,
        )

    def send_mat(n):
        peer = jnp.where(n % 2 == 0, g + 1, g - 1)
        return pltpu.make_async_remote_copy(
            sm.at[n], rm.at[n, core], th_ss.at[1, n], th_rs.at[1, n],
            device_id=dev(peer, j), device_id_type=MESH,
        )

    def forward(n):
        return pltpu.make_async_remote_copy(
            rm.at[n, core], rm.at[n, core], fw_ss.at[n], fw_rs.at[n],
            device_id=dev(g, j + 1 - 2 * core), device_id_type=MESH,
        )

    def pass_on(n):
        @pl.when(has_in(n))
        def _():
            send_mat(n).wait_recv()
            forward(n).start()

    def send_vol(d):
        peer = jnp.where(d == 0, g + 1, g - 1)
        return pltpu.make_async_remote_copy(
            sv.at[d], rv.at[d], tv_ss.at[d], tv_rs.at[d],
            device_id=dev(peer, j), device_id_type=MESH,
        )

    def group1(o, src, dst, u):
        return pltpu.make_async_remote_copy(
            src, dst.at[o], g_ss.at[u, o], g_rs.at[u, o],
            device_id=dev(g, z * WN + (w + o) % WN), device_id_type=MESH,
        )

    def group2(o, src, dst, u):
        return pltpu.make_async_remote_copy(
            src, dst.at[o], g_ss.at[u, o], g_rs.at[u, o],
            device_id=dev(g, ((z + o) % 8) * WN + w), device_id_type=MESH,
        )

    lax.fori_loop(0, 4, fill, 0)
    pl.semaphore_wait(
        barrier, 16 + jnp.where(g > 0, 1, 0) + jnp.where(g < TN - 1, 1, 0)
    )
    for o in range(1, WN):
        group1(o, ctile, g1, 0).start()

    def each_dir(fn):
        @pl.when(g < TN - 1)
        def _():
            fn(0)

        @pl.when(g > 0)
        def _():
            fn(1)

    def has_in(n):
        return jnp.where(n % 2 == 0, g > 0, g < TN - 1)

    def has_out(n):
        return jnp.where(n % 2 == 0, g < TN - 1, g > 0)

    each_dir(lambda d: send_vol(d).start())

    def start_mat(n, _):
        @pl.when(has_out(n))
        def _():
            send_mat(n).start()

        return 0

    def start_copy(n, _):
        @pl.when(has_out(n))
        def _():
            send_copy(n).start()

        return 0

    lax.fori_loop(0, 4, start_mat, 0)
    lax.fori_loop(0, 2, start_copy, 0)
    lax.fori_loop(4, 2 * KEEP, fill, 0)

    def start_more(r, _):
        for d in range(2):
            start_mat(2 * r + 2 + d, 0)
        for d in range(2):
            start_copy(2 * r + d, 0)
        return 0

    lax.fori_loop(1, KEEP - 1, start_more, 0)

    def request(side):
        return pltpu.make_async_remote_copy(
            req.at[side], reqin.at[side], rq_ss.at[side], rq_rs.at[side],
            device_id=dev(g - 1 if side == 0 else g + 1, j), device_id_type=MESH,
        )

    def request_any(d):
        return pltpu.make_async_remote_copy(
            req.at[d], reqin.at[d], rq_ss.at[d], rq_rs.at[d],
            device_id=dev(jnp.where(d == 0, g - 1, g + 1), j), device_id_type=MESH,
        )

    def send_drawn(d):
        return pltpu.make_async_remote_copy(
            own.at[PD + d], rcT.at[d], th_ss.at[0, LAST + d], th_rs.at[0, LAST + d],
            device_id=dev(jnp.where(d == 0, g + 1, g - 1), j), device_id_type=MESH,
        )

    takes = (g > 0, g < TN - 1)
    gives = (g < TN - 1, g > 0)

    eyer[...] = eye(K)
    lines[...] = iota((256, 256), 0).astype(F32).astype(BF16)
    load_nz.wait()
    for t in range(STEPS):
        nT[t] = nt(eyer[...], nz[t]).astype(BF16)
        yb[t] = jnp.transpose(jnp.broadcast_to(yl[t : t + 1, :], (M, M)))
    lT[...] = nt(eye(M), ld[...]).astype(BF16)
    stats[...] = jnp.zeros_like(stats)

    before = jnp.zeros((PD, 128), I32)
    whole = ctile[...]
    for o in range(1, WN):
        group1(o, ctile, g1, 0).wait_recv()
        got = g1[o]
        source = (w + WN - o) % WN
        before = before + jnp.where(source < w, got, 0)
        whole = whole + got
    c2tile[...] = whole
    for o in range(1, 8):
        group2(o, c2tile, g2, 1).start()
    for o in range(1, 8):
        group2(o, c2tile, g2, 1).wait_recv()
        source = (z + 8 - o) % 8
        before = before + jnp.where(source < z, g2[o], 0)
    first = before - SD * j
    for t in range(STEPS):
        d = jnp.broadcast_to(first[:, t : t + 1], (PD, 128))
        e = d + jnp.broadcast_to(tile[:, t : t + 1], (PD, 128))
        dref[t * PD : (t + 1) * PD, :] = d
        eref[t * PD : (t + 1) * PD, :] = e
        shift = jnp.concatenate([d + MARGIN] * (FRAME // 128), axis=1)
        x = la[t * PD : (t + 1) * PD, :]
        for b in range(9):
            x = jnp.where((shift & (1 << b)) != 0, pltpu.roll(x, 1 << b, 1), x)
        cz[t * PD : (t + 1) * PD, :] = x

    def halo(n, t):
        to_left = pltpu.make_async_remote_copy(
            eL.at[n, t], hR.at[n, t], hl_ss.at[0, n, t], hl_rs.at[0, n, t],
            device_id=dev(g, left), device_id_type=MESH,
        )
        to_right = pltpu.make_async_remote_copy(
            eR.at[n, t], hL.at[n, t], hl_ss.at[1, n, t], hl_rs.at[1, n, t],
            device_id=dev(g, right), device_id_type=MESH,
        )
        return to_left, to_right

    def arrive(n):
        @pl.when(has_in(n))
        def _():
            send_copy(n).wait_recv()
            forward(n).wait_recv()

        pass_on(n + 2)

    def put_cloud(n, cloud, vol):
        cT[n, 0:K, :] = nt(eyer[...], cloud).astype(BF16)
        cT[n, K:EXT, :] = jnp.broadcast_to(vol, (EXT - K, SD)).astype(BF16)

    def build_mat(n):
        got = jnp.concatenate([rm[n, 0], rm[n, 1]], axis=0).astype(F32)
        mat = jnp.where(rem_s[n] == 1, got, tr[src_s[n]].astype(F32)).astype(BF16)
        mT[n] = nt(eyer[...], mat).astype(BF16)

    def build(n):
        src = src_s[n]
        remote = rem_s[n] == 1
        cloud = jnp.where(remote, rc[n].astype(F32), st[src].astype(F32)).astype(BF16)
        got = rv[n % 2, pl.ds(n // 2, 1), :]
        put_cloud(n, cloud, jnp.where(remote, got, lvf[pl.ds(src, 1), :]))
        build_mat(n)

    def row_of(n, t):
        return jnp.where(n < PD, t * PD + perm_s[jnp.minimum(n, PD - 1)], STEPS * PD + n - PD)

    def picks_of(n, t):
        return cz[pl.ds(row_of(n, t), 1), :]

    def draw(ns, t, tables):
        rows = lines[...]
        picks = [picks_of(n, t).astype(F32) for n in ns]
        out = []
        for b in range(FRAME // 256):
            hots = []
            for pick in picks:
                row = pick[:, b * 256 : (b + 1) * 256]
                hots.append(
                    jnp.concatenate(
                        [
                            jnp.where(
                                rows == (row - float(part * 256)).astype(BF16),
                                jnp.ones((), BF16),
                                jnp.zeros((), BF16),
                            )
                            for part in range(2)
                        ],
                        axis=0,
                    )
                )
            out.append([nn(x, hot).astype(BF16) for x, hot in zip(tables, hots)])
        for i, n in enumerate(ns):
            eL[n, t] = out[0][i][:, 0:MARGIN]
            eR[n, t] = out[2][i][:, MARGIN:256]
        for i, n in enumerate(ns):
            own[n, :, 0:128] = out[0][i][:, MARGIN:256]
            own[n, :, 128:384] = out[1][i]
            own[n, :, 384:512] = out[2][i][:, 0:MARGIN]

    def send_halo(n, t):
        for copy in halo(n, t):
            copy.start()

    def wait_halo(n, t):
        for copy in halo(n, t):
            copy.wait_recv()

    def merge_with(n, t, d, e):
        lane = iota((1, 128), 1)
        front = jnp.where(
            lane < d, hL[n, t].astype(F32), own[n, :, 0:128].astype(F32)
        ).astype(BF16)
        back = jnp.where(
            lane + 384 >= e, hR[n, t].astype(F32), own[n, :, 384:512].astype(F32)
        ).astype(BF16)
        own[n, :, 0:128] = front
        own[n, :, 384:512] = back

    def merge(n, t):
        at = row_of(n, t)
        merge_with(n, t, dref[pl.ds(at, 1), :], eref[pl.ds(at, 1), :])

    def step(ns, t):
        lane = iota((1, 128), 1)
        halves = [slice(b * 256, (b + 1) * 256) for b in range(2)]
        xs = [[own[n, :, c] for c in halves] for n in ns]
        mats = [mT[n] for n in ns]
        noise_t = [nT[t, :, c].astype(F32) for c in halves]
        shocks = [vn[pl.ds(t, 1), c] for c in halves]
        y = yb[t]
        y = jnp.concatenate([y, y], axis=1)
        load = lT[...]
        clouds, hs = [], []
        for n, x, mat in zip(ns, xs, mats):
            a = anc_s[n]
            center, persist, spread = vm_s[a], vp_s[a], vs_s[a]
            cloud, level = [], []
            for b in range(2):
                vol = x[b][K:EXT].astype(F32)[0:1]
                h = center + persist * (vol - center) + spread * shocks[b]
                drift = nn(mat, x[b][0:K])
                cloud.append((drift + jnp.exp(0.5 * h) * noise_t[b]).astype(BF16))
                level.append(h)
            clouds.append(cloud)
            hs.append(level)
        tables = []
        for n, cloud, level in zip(ns, clouds, hs):
            h = jnp.concatenate(level, axis=1)
            cT[n, 0:K, 0:256] = cloud[0]
            cT[n, 0:K, 256:512] = cloud[1]
            o_vol[pl.ds(n, 1), :] = h.astype(BF16).astype(F32)
            wide = jnp.broadcast_to(h, (EXT - K, SD)).astype(BF16)
            tables.append(
                jnp.concatenate([jnp.concatenate(cloud, axis=1), wide], axis=0)
            )

        def weigh():
            for n, cloud in zip(ns, clouds):
                prec = op_s[anc_s[n]]
                parts = []
                for b in range(2):
                    miss = y - nn(load, cloud[b])
                    ssq = jnp.sum(miss * miss, axis=0, keepdims=True)
                    parts.append(-0.5 * prec * ssq)
                logw = jnp.concatenate(parts, axis=1)
                logw = logw + 0.5 * M * jnp.log(jnp.full((1, 1), prec, F32))
                peak = jnp.max(logw, axis=1, keepdims=True)
                mass = jnp.sum(jnp.exp(logw - peak), axis=1, keepdims=True)
                here = lane == t
                for at, value in ((n, peak), (PD + n, mass)):
                    old = stats[pl.ds(at, 1), :]
                    stats[pl.ds(at, 1), :] = jnp.where(here, value, old)

        return tables, weigh

    def finish(n):
        for b in range(2):
            block = cT[n, 0:K, b * 256 : (b + 1) * 256]
            osb[n, b * 256 : (b + 1) * 256, :] = nt(eyer[...], block).astype(BF16)
        pltpu.make_async_copy(osb.at[n], o_states.at[n], out_sem.at[n]).start()

    def ask():
        for side in range(2):
            n = LAST + side
            row = picks_of(n, 0)
            for b in range(FRAME // 128):
                req[side, b : b + 1, :] = row[:, b * 128 : (b + 1) * 128]
            req[side, 6:7, :] = dref[pl.ds(perm_s[n], 1), :]
            req[side, 7:8, :] = eref[pl.ds(perm_s[n], 1), :]
        for side in range(2):
            @pl.when(takes[side])
            def _(side=side):
                request(side).start()

        for side in range(2):
            src = src_s[LAST + side]
            put_cloud(LAST + side, st[src], lvf[pl.ds(src, 1), :])
        draw((LAST, LAST + 1), 0, [cT[LAST], cT[LAST + 1]])
        send_halo(LAST, 0)
        send_halo(LAST + 1, 0)

    def take_request(d):
        @pl.when(gives[d])
        def _():
            request_any(d).wait_recv()

        at = STEPS * PD + d
        cz[pl.ds(at, 1), :] = jnp.concatenate(
            [reqin[d, b : b + 1, :] for b in range(FRAME // 128)], axis=1
        )
        dref[pl.ds(at, 1), :] = reqin[d, 6:7, :]
        eref[pl.ds(at, 1), :] = reqin[d, 7:8, :]

    def task(m, _):
        code = PACKED[0]
        for k in range(1, len(PACKED)):
            code = jnp.where(m // 4 == k, PACKED[k], code)
        code = lax.shift_right_logical(code, 7 * (m % 4)) & 127
        kind, r, t = code // 16, (code // 4) % 4, code % 4
        pair = (2 * r, 2 * r + 1)
        late = (r == KEEP - 1) & (t == 0)

        @pl.when(kind == BUILD)
        def _():
            for n in pair:
                arrive(n)
            for n in pair:
                build(n)
            draw(pair, 0, [cT[n] for n in pair])
            for n in pair:
                send_halo(n, 0)

        @pl.when(kind == SERVE)
        def _():
            for d in range(2):
                take_request(d)
            for d in range(2):
                put_cloud(PD + d, sc[LAST + d], sv[d, KEEP - 1 : KEEP, :])
            draw((PD, PD + 1), 0, [cT[PD], cT[PD + 1]])
            for d in range(2):
                send_halo(PD + d, 0)

        @pl.when(kind == PASS)
        def _():
            for d in range(2):
                wait_halo(PD + d, 0)
            for d in range(2):
                merge(PD + d, 0)
            for d in range(2):
                @pl.when(gives[d])
                def _(d=d):
                    send_drawn(d).start()

            for n in (LAST, LAST + 1):
                wait_halo(n, 0)
            for n in (LAST, LAST + 1):
                merge(n, 0)

        @pl.when((kind == GO) & late)
        def _():
            for side in range(2):
                @pl.when(takes[side])
                def _(side=side):
                    forward(LAST + side).wait_recv()
                    send_drawn(side).wait_recv()

            for side in range(2):
                n = LAST + side
                build_mat(n)
                own[n] = jnp.where(
                    rem_s[n] == 1, rcT[side].astype(F32), own[n].astype(F32)
                ).astype(BF16)

        @pl.when(((kind == GO) | (kind == END)) & jnp.logical_not(late))
        def _():
            for n in pair:
                wait_halo(n, t)
            for n in pair:
                merge(n, t)

        @pl.when(kind == GO)
        def _():
            tables, weigh = step(pair, t)
            draw(pair, t + 1, tables)
            for n in pair:
                send_halo(n, t + 1)
            weigh()

        @pl.when(kind == END)
        def _():
            step(pair, t)[1]()

        @pl.when((kind == END) & (r < 2))
        def _():
            for n in pair:
                finish(n)

        return 0

    each_in = ((g > 0, 0), (g < TN - 1, 1))
    for cond, d in each_in:
        @pl.when(cond)
        def _(d=d):
            send_vol(d).wait_recv()

    ask()
    pass_on(0)
    pass_on(1)
    lax.fori_loop(0, len(ORDER), task, 0)

    def join(buf, here):
        order = [buf[(here + 8 - k) % 8] for k in range(8)]
        peak = order[0][0:PD]
        for x in order[1:]:
            peak = jnp.maximum(peak, x[0:PD])
        mass = jnp.zeros((PD, 128), F32)
        for x in order:
            mass = mass + x[PD:] * jnp.exp(x[0:PD] - peak)
        return peak, mass

    s1[0] = stats[...]
    for o in range(1, WN):
        group1(o, stats, s1, 2).start()

    for n in range(LAST - 2, PD):
        finish(n)
    for o in range(1, WN):
        group1(o, stats, s1, 2).wait_recv()
    peak, mass = join(s1, w)
    s2[0, 0:PD, :] = peak
    s2[0, PD:, :] = mass
    for o in range(1, 8):
        group2(o, s2.at[0], s2, 3).start()
    for o in range(1, 8):
        group2(o, s2.at[0], s2, 3).wait_recv()
    peak, mass = join(s2, z)
    live = lane8 < STEPS
    part = peak + jnp.log(jnp.where(live, mass, 1.0)) - math.log(SD * JN)
    total = jnp.sum(jnp.where(live, part, 0.0), axis=1, keepdims=True)
    o_ll[...] = jnp.broadcast_to(total, (PD, 128))

    for o in range(1, WN):
        group1(o, ctile, g1, 0).wait_send()
        group2(o, c2tile, g2, 1).wait_send()
        group1(o, stats, s1, 2).wait_send()
        group2(o, s2.at[0], s2, 3).wait_send()
    each_dir(lambda d: send_vol(d).wait_send())

    for d in range(2):
        @pl.when(gives[d])
        def _(d=d):
            send_drawn(d).wait_send()

        @pl.when(takes[d])
        def _(d=d):
            request(d).wait_send()

        for copy in halo(PD + d, 0):
            copy.wait_send()

    def drain(n, _):
        @pl.when(has_out(n))
        def _():
            send_mat(n).wait_send()

        @pl.when(has_out(n) & (n < LAST))
        def _():
            send_copy(n).wait_send()

        @pl.when(has_in(n))
        def _():
            forward(n).wait_send()

        def drain_t(t, _):
            to_left, to_right = halo(n, t)
            to_left.wait_send()
            to_right.wait_send()
            return 0

        lax.fori_loop(0, STEPS, drain_t, 0)
        pltpu.make_async_copy(osb.at[n], o_states.at[n], out_sem.at[n]).wait()
        return 0

    lax.fori_loop(0, PD, drain, 0)


def reorder(anc, pos, pr_s, res, vol, ll, o_states, o_vol, o_ll, buf, rows, sem):
    g = lax.axis_index("theta")

    def take(i):
        return pltpu.make_async_copy(res.at[pos[i]], buf.at[i], sem.at[0, i])

    def give(i):
        return pltpu.make_async_copy(buf.at[i], o_states.at[i], sem.at[1, i])

    for i in range(PD):
        take(i).start()
    lane = iota((1, 128), 1)
    out = jnp.zeros((1, 128), F32)
    for i in range(PD):
        rows[i : i + 1, :] = vol[pl.ds(pos[i], 1), :]
        value = ll[pl.ds(pos[i], 1), :] + pr_s[anc[g * PD + i]]
        out = jnp.where(lane == i, value, out)
    o_vol[...] = rows[...].astype(BF16)
    o_ll[...] = out[:, 0:PD]
    for i in range(PD):
        take(i).wait()
        give(i).start()
    for i in range(PD):
        give(i).wait()


def local(
    states, log_vol, transition, loading, yields, state_noise, vol_noise,
    vol_mean, vol_persist, vol_scale, obs_prec, prior_loglik,
    ancestors, counts, local_anc,
):
    smem = pl.BlockSpec(memory_space=pltpu.SMEM)
    vmem = pl.BlockSpec(memory_space=pltpu.VMEM)
    hbm = pl.BlockSpec(memory_space=pl.ANY)
    dma = pltpu.SemaphoreType.DMA
    v, s = pltpu.VMEM, pltpu.SMEM
    res, vol, ll, pos = pl.pallas_call(
        kernel,
        out_shape=(
            jax.ShapeDtypeStruct((PD, SD, K), BF16),
            jax.ShapeDtypeStruct((PD, SD), F32),
            jax.ShapeDtypeStruct((PD, 128), F32),
            jax.ShapeDtypeStruct((PD,), I32),
        ),
        in_specs=[smem] * 6 + [vmem] * 6 + [hbm] * 3,
        out_specs=(hbm, vmem, vmem, smem),
        scratch_shapes=[
            v((PD, SD, K), BF16), v((PD, K, K), BF16), v((STEPS, SD, K), BF16),
            v((PD, SD, K), BF16), v((PD, HALF, K), BF16), v((2, PD, SD), F32),
            v((PD, SD, K), BF16), v((PD, 2, HALF, K), BF16), v((2, PD, SD), F32),
            v((2, EXT, SD), BF16), v((2, 8, 128), I32), v((2, 8, 128), I32),
            v((PD + 2, EXT, SD), BF16), v((PD + 2, EXT, SD), BF16), v((PD, K, K), BF16),
            v((STEPS, K, SD), BF16), v((M, K), BF16), v((STEPS, M, M), F32),
            v((PD + 2, STEPS, EXT, MARGIN), BF16), v((PD + 2, STEPS, EXT, MARGIN), BF16),
            v((PD + 2, STEPS, EXT, MARGIN), BF16), v((PD + 2, STEPS, EXT, MARGIN), BF16),
            v((PD, 128), I32), v((PD, 128), I32),
            v((8, PD, 128), I32), v((8, PD, 128), I32),
            v((STEPS * PD + 8, 128), I32), v((STEPS * PD + 8, 128), I32),
            v((STEPS * PD + 8, FRAME), I32),
            v((2 * PD, 128), F32), v((8, 2 * PD, 128), F32), v((8, 2 * PD, 128), F32),
            v((PD, SD), F32), v((PD, SD, K), BF16), v((K, K), BF16), v((256, 256), BF16),
            s((PD,), I32), s((PD,), I32), s((PD,), I32), s((PD,), I32), s((PD,), I32),
            dma((3,)), dma((2, PD)), dma((2, PD)), dma((2,)), dma((2,)), dma((PD,)), dma((PD,)),
            dma((2,)), dma((2,)), dma((2, PD + 2, STEPS)), dma((2, PD + 2, STEPS)),
            dma((4, 8)), dma((4, 8)), dma((PD,)),
        ],
        compiler_params=pltpu.CompilerParams(
            collective_id=0, has_side_effects=True, vmem_limit_bytes=63 << 20
        ),
    )(
        ancestors, vol_mean, vol_persist, vol_scale, obs_prec, prior_loglik,
        counts.transpose(0, 2, 1), log_vol, loading, yields, vol_noise,
        local_anc.reshape(STEPS * PD, FRAME), states, transition, state_noise,
    )
    final, final_vol, loglik = pl.pallas_call(
        reorder,
        out_shape=(
            jax.ShapeDtypeStruct((PD, SD, K), BF16),
            jax.ShapeDtypeStruct((PD, SD), BF16),
            jax.ShapeDtypeStruct((1, PD), F32),
        ),
        in_specs=[smem] * 3 + [hbm, vmem, vmem],
        out_specs=(hbm, vmem, vmem),
        scratch_shapes=[v((PD, SD, K), BF16), v((PD, SD), F32), dma((2, PD))],
        compiler_params=pltpu.CompilerParams(vmem_limit_bytes=63 << 20),
    )(ancestors, pos, prior_loglik, res, vol, ll)
    return final, final_vol, loglik.reshape(PD)


def solution(mesh):
    placed = (
        P("theta", "state", None),
        P("theta", "state"),
        P("theta", None, None),
        P(),
        P(),
        P(None, "state", None),
        P(None, "state"),
        P(),
        P(),
        P(),
        P(),
        P(),
        P(),
        P(None, "theta", "state"),
        P(None, "theta", "state"),
    )
    return jax.shard_map(
        local,
        mesh=mesh,
        in_specs=placed,
        out_specs=(P("theta", "state", None), P("theta", "state"), P("theta")),
        check_vma=False,
    )
```

```python
import math

import jax
import jax.numpy as jnp
from jax import lax
from jax.experimental import pallas as pl
from jax.experimental.pallas import tpu as pltpu
from jax.sharding import PartitionSpec as P

K = 256
M = 128
PD = 8
SD = 512
STEPS = 3
MARGIN = 128
FRAME = SD + 2 * MARGIN
EXT = K + 16
HALF = K // 2
Q = 2
ROWS = HALF // Q
KEEP = 4
LAST = 2 * KEEP - 2
TN = 4
JN = 64
WN = 8
BUILD, GO, END, SERVE, PASS = range(5)
ORDER = (
    (BUILD, 0, 0), (GO, 0, 0), (BUILD, 1, 0), (SERVE, 0, 0), (GO, 0, 1), (GO, 1, 0), (PASS, 0, 0), (BUILD, 2, 0), (END, 0, 2), (GO, 1, 1), (GO, 2, 0), (GO, 3, 0), (END, 1, 2), (GO, 2, 1), (GO, 3, 1), (END, 2, 2), (END, 3, 2),
)
PACKED = [
    sum((16 * k + 4 * r + t) << (7 * i) for i, (k, r, t) in enumerate(ORDER[at : at + 4]))
    for at in range(0, len(ORDER), 4)
]
F32 = jnp.float32
BF16 = jnp.bfloat16
I32 = jnp.int32
MESH = pl.DeviceIdType.MESH


def nt(a, b):
    return lax.dot_general(a, b, (((1,), (1,)), ((), ())), preferred_element_type=F32)


def nn(a, b):
    return lax.dot_general(a, b, (((1,), (0,)), ((), ())), preferred_element_type=F32)


def iota(shape, dim):
    return lax.broadcasted_iota(I32, shape, dim)


def eye(n):
    return jnp.where(iota((n, n), 0) == iota((n, n), 1), 1.0, 0.0).astype(BF16)


def kernel(
    anc, vm_s, vp_s, vs_s, op_s, pr_s,
    cnt, lv, ld, yl, vn, la, states, trans, noise,
    o_states, o_vol, o_ll, o_pos,
    st, tr, nz, sc, sm, sv, rc, rm, rv, rcT, req, reqin,
    cT, own, mT, nT, lT, yb, eL, eR, hL, hR,
    ctile, c2tile, g1, g2, dref, eref, cz, stats, s1, s2, lvf, osb, eyer, lines,
    perm_s, src_s, rem_s, anc_s, snd_s,
    ld_sem, th_ss, th_rs, rq_ss, rq_rs, zf_ss, zf_rs, fw_ss, fw_rs, tv_ss, tv_rs, hl_ss, hl_rs, g_ss, g_rs, out_sem,
):
    g = lax.axis_index("theta")
    j = lax.axis_index("state")
    z, w, core = j // WN, j % WN, j % 2
    zq = z % Q
    left, right = (j + JN - 1) % JN, (j + 1) % JN

    def dev(theta, state):
        return {"theta": theta, "state": state}

    barrier = pltpu.get_barrier_semaphore()

    def greet(theta, state):
        pl.semaphore_signal(
            barrier, inc=1, device_id=dev(theta, state), device_id_type=MESH
        )

    for o in range(1, 8):
        greet(g, ((z + o) % 8) * WN + w)
    for o in range(1, WN):
        greet(g, z * WN + (w + o) % WN)
    greet(g, left)
    greet(g, right)

    @pl.when(g > 0)
    def _():
        greet(g - 1, j)

    @pl.when(g < TN - 1)
    def _():
        greet(g + 1, j)

    load_st = pltpu.make_async_copy(states, st, ld_sem.at[0])
    load_tr = pltpu.make_async_copy(trans, tr, ld_sem.at[1])
    load_nz = pltpu.make_async_copy(noise, nz, ld_sem.at[2])
    load_st.start()
    load_tr.start()
    load_nz.start()

    a8 = [anc[g * PD + i] for i in range(PD)]
    off = [lax.shift_right_arithmetic(a, 3) - g for a in a8]
    below = [jnp.where(o == -1, 1, 0) for o in off]
    above = [jnp.where(o == 1, 1, 0) for o in off]
    nb, na, nl = 0, 0, 0
    rank_b, rank_a, rank_l = [], [], []
    for i in range(PD):
        rank_b.append(nb)
        rank_a.append(na)
        rank_l.append(nl)
        nb = nb + below[i]
        na = na + above[i]
        nl = nl + 1 - below[i] - above[i]
    free_b = KEEP - nb
    pos = []
    for i in range(PD):
        l = rank_l[i]
        home = jnp.where(l < free_b, 2 * (nb + l), 2 * (na + l - free_b) + 1)
        slot = jnp.where(
            below[i] == 1,
            2 * rank_b[i],
            jnp.where(above[i] == 1, 2 * rank_a[i] + 1, home),
        )
        pos.append(jnp.clip(slot, 0, PD - 1))
        o_pos[i] = pos[i]
    for n in range(PD):
        who, a = 0, 0
        for i in range(PD):
            hit = pos[i] == n
            who = jnp.where(hit, i, who)
            a = jnp.where(hit, a8[i], a)
        perm_s[n] = who
        anc_s[n] = a
        src_s[n] = a & (PD - 1)
        rem_s[n] = jnp.where(lax.shift_right_arithmetic(a, 3) == g, 0, 1)
    for d, peer in ((0, jnp.minimum(g + 1, TN - 1)), (1, jnp.maximum(g - 1, 0))):
        rank = 0
        chosen = [0] * KEEP
        for i in range(PD):
            a = anc[peer * PD + i]
            hit = jnp.where(lax.shift_right_arithmetic(a, 3) == g, 1, 0)
            for k in range(KEEP):
                take = jnp.where(rank == k, hit, 0)
                chosen[k] = jnp.where(take == 1, a & (PD - 1), chosen[k])
            rank = rank + hit
        for k in range(KEEP):
            snd_s[2 * k + d] = chosen[k]

    lane8 = iota((PD, 128), 1)
    tile = jnp.zeros((PD, 128), I32)
    for t in range(STEPS):
        line = jnp.broadcast_to(cnt[t].astype(F32), (PD, PD))
        line = jnp.where(iota((PD, PD), 0) == iota((PD, PD), 1), line, 0.0)
        column = jnp.sum(line, axis=1, keepdims=True).astype(I32)
        tile = jnp.where(lane8 == t, jnp.broadcast_to(column, (PD, 128)), tile)
    ctile[...] = tile
    lvf[...] = lv[...].astype(F32)
    for d in range(2):
        for k in range(KEEP):
            row = lvf[pl.ds(snd_s[2 * k + d], 1), :]
            sv[d, k : k + 1, :] = row
            sv[d, KEEP + k : KEEP + k + 1, :] = row
    load_st.wait()
    load_tr.wait()

    def fill(n, _):
        s = snd_s[n]
        sc[n] = st[s]
        sm[n] = tr[s, pl.ds(pl.multiple_of(core * HALF + zq * ROWS, ROWS), ROWS), :]
        return 0

    def send_copy(n):
        peer = jnp.where(n % 2 == 0, g + 1, g - 1)
        return pltpu.make_async_remote_copy(
            sc.at[n], rc.at[n], th_ss.at[0, n], th_rs.at[0, n],
            device_id=dev(peer, j), device_id_type=MESH,
        )

    def send_mat(n):
        peer = jnp.where(n % 2 == 0, g + 1, g - 1)
        return pltpu.make_async_remote_copy(
            sm.at[n], rm.at[n, core, zq], th_ss.at[1, n], th_rs.at[1, n],
            device_id=dev(peer, j), device_id_type=MESH,
        )

    def forward(n):
        return pltpu.make_async_remote_copy(
            rm.at[n, core], rm.at[n, core], fw_ss.at[n], fw_rs.at[n],
            device_id=dev(g, j + 1 - 2 * core), device_id_type=MESH,
        )

    def spread(n, o):
        return pltpu.make_async_remote_copy(
            rm.at[n, core, zq], rm.at[n, core, zq], zf_ss.at[n, o], zf_rs.at[n, o],
            device_id=dev(g, (z - zq + (zq + o) % Q) * WN + w), device_id_type=MESH,
        )

    def pass_on(n):
        @pl.when(has_in(n))
        def _():
            send_mat(n).wait_recv()
            for o in range(1, Q):
                spread(n, o).start()

    def pass_two(n):
        @pl.when(has_in(n))
        def _():
            for o in range(1, Q):
                came = rm.at[n, core, (zq + Q - o) % Q]
                pltpu.make_async_remote_copy(
                    came, came, zf_ss.at[n, o], zf_rs.at[n, o],
                    device_id=dev(g, (z - zq + (zq + o) % Q) * WN + w),
                    device_id_type=MESH,
                ).wait_recv()
            forward(n).start()

    def send_vol(d):
        peer = jnp.where(d == 0, g + 1, g - 1)
        return pltpu.make_async_remote_copy(
            sv.at[d], rv.at[d], tv_ss.at[d], tv_rs.at[d],
            device_id=dev(peer, j), device_id_type=MESH,
        )

    def group1(o, src, dst, u):
        return pltpu.make_async_remote_copy(
            src, dst.at[o], g_ss.at[u, o], g_rs.at[u, o],
            device_id=dev(g, z * WN + (w + o) % WN), device_id_type=MESH,
        )

    def group2(o, src, dst, u):
        return pltpu.make_async_remote_copy(
            src, dst.at[o], g_ss.at[u, o], g_rs.at[u, o],
            device_id=dev(g, ((z + o) % 8) * WN + w), device_id_type=MESH,
        )

    lax.fori_loop(0, 4, fill, 0)
    pl.semaphore_wait(
        barrier, 16 + jnp.where(g > 0, 1, 0) + jnp.where(g < TN - 1, 1, 0)
    )
    for o in range(1, WN):
        group1(o, ctile, g1, 0).start()

    def each_dir(fn):
        @pl.when(g < TN - 1)
        def _():
            fn(0)

        @pl.when(g > 0)
        def _():
            fn(1)

    def has_in(n):
        return jnp.where(n % 2 == 0, g > 0, g < TN - 1)

    def has_out(n):
        return jnp.where(n % 2 == 0, g < TN - 1, g > 0)

    each_dir(lambda d: send_vol(d).start())

    def start_mat(n, _):
        @pl.when(has_out(n))
        def _():
            send_mat(n).start()

        return 0

    def start_copy(n, _):
        @pl.when(has_out(n))
        def _():
            send_copy(n).start()

        return 0

    lax.fori_loop(0, 4, start_mat, 0)
    lax.fori_loop(0, 2, start_copy, 0)
    lax.fori_loop(4, 2 * KEEP, fill, 0)

    def start_more(r, _):
        for d in range(2):
            start_mat(2 * r + 2 + d, 0)
        for d in range(2):
            start_copy(2 * r + d, 0)
        return 0

    lax.fori_loop(1, KEEP - 1, start_more, 0)

    def request(side):
        return pltpu.make_async_remote_copy(
            req.at[side], reqin.at[side], rq_ss.at[side], rq_rs.at[side],
            device_id=dev(g - 1 if side == 0 else g + 1, j), device_id_type=MESH,
        )

    def request_any(d):
        return pltpu.make_async_remote_copy(
            req.at[d], reqin.at[d], rq_ss.at[d], rq_rs.at[d],
            device_id=dev(jnp.where(d == 0, g - 1, g + 1), j), device_id_type=MESH,
        )

    def send_drawn(d):
        return pltpu.make_async_remote_copy(
            own.at[PD + d], rcT.at[d], th_ss.at[0, LAST + d], th_rs.at[0, LAST + d],
            device_id=dev(jnp.where(d == 0, g + 1, g - 1), j), device_id_type=MESH,
        )

    takes = (g > 0, g < TN - 1)
    gives = (g < TN - 1, g > 0)

    eyer[...] = eye(K)
    lines[...] = iota((256, 256), 0).astype(F32).astype(BF16)
    load_nz.wait()
    for t in range(STEPS):
        nT[t] = nt(eyer[...], nz[t]).astype(BF16)
        yb[t] = jnp.transpose(jnp.broadcast_to(yl[t : t + 1, :], (M, M)))
    lT[...] = nt(eye(M), ld[...]).astype(BF16)
    stats[...] = jnp.zeros_like(stats)

    before = jnp.zeros((PD, 128), I32)
    whole = ctile[...]
    for o in range(1, WN):
        group1(o, ctile, g1, 0).wait_recv()
        got = g1[o]
        source = (w + WN - o) % WN
        before = before + jnp.where(source < w, got, 0)
        whole = whole + got
    c2tile[...] = whole
    for o in range(1, 8):
        group2(o, c2tile, g2, 1).start()
    for o in range(1, 8):
        group2(o, c2tile, g2, 1).wait_recv()
        source = (z + 8 - o) % 8
        before = before + jnp.where(source < z, g2[o], 0)
    first = before - SD * j
    for t in range(STEPS):
        d = jnp.broadcast_to(first[:, t : t + 1], (PD, 128))
        e = d + jnp.broadcast_to(tile[:, t : t + 1], (PD, 128))
        dref[t * PD : (t + 1) * PD, :] = d
        eref[t * PD : (t + 1) * PD, :] = e
        shift = jnp.concatenate([d + MARGIN] * (FRAME // 128), axis=1)
        x = la[t * PD : (t + 1) * PD, :]
        for b in range(9):
            x = jnp.where((shift & (1 << b)) != 0, pltpu.roll(x, 1 << b, 1), x)
        cz[t * PD : (t + 1) * PD, :] = x

    def halo(n, t):
        to_left = pltpu.make_async_remote_copy(
            eL.at[n, t], hR.at[n, t], hl_ss.at[0, n, t], hl_rs.at[0, n, t],
            device_id=dev(g, left), device_id_type=MESH,
        )
        to_right = pltpu.make_async_remote_copy(
            eR.at[n, t], hL.at[n, t], hl_ss.at[1, n, t], hl_rs.at[1, n, t],
            device_id=dev(g, right), device_id_type=MESH,
        )
        return to_left, to_right

    def arrive(n):
        @pl.when(has_in(n))
        def _():
            send_copy(n).wait_recv()


    def put_cloud(n, cloud, vol):
        cT[n, 0:K, :] = nt(eyer[...], cloud).astype(BF16)
        cT[n, K:EXT, :] = jnp.broadcast_to(vol, (EXT - K, SD)).astype(BF16)

    def build_mat(n):
        @pl.when(has_in(n))
        def _():
            forward(n).wait_recv()

        pieces = [rm[n, c, q] for c in range(2) for q in range(Q)]
        got = jnp.concatenate(pieces, axis=0).astype(F32)
        mat = jnp.where(rem_s[n] == 1, got, tr[src_s[n]].astype(F32)).astype(BF16)
        mT[n] = nt(eyer[...], mat).astype(BF16)

    def build(n):
        src = src_s[n]
        remote = rem_s[n] == 1
        cloud = jnp.where(remote, rc[n].astype(F32), st[src].astype(F32)).astype(BF16)
        got = rv[n % 2, pl.ds(n // 2, 1), :]
        put_cloud(n, cloud, jnp.where(remote, got, lvf[pl.ds(src, 1), :]))

    def row_of(n, t):
        return jnp.where(n < PD, t * PD + perm_s[jnp.minimum(n, PD - 1)], STEPS * PD + n - PD)

    def picks_of(n, t):
        return cz[pl.ds(row_of(n, t), 1), :]

    def draw(ns, t, tables):
        rows = lines[...]
        picks = [picks_of(n, t).astype(F32) for n in ns]
        out = []
        for b in range(FRAME // 256):
            hots = []
            for pick in picks:
                row = pick[:, b * 256 : (b + 1) * 256]
                hots.append(
                    jnp.concatenate(
                        [
                            jnp.where(
                                rows == (row - float(part * 256)).astype(BF16),
                                jnp.ones((), BF16),
                                jnp.zeros((), BF16),
                            )
                            for part in range(2)
                        ],
                        axis=0,
                    )
                )
            out.append([nn(x, hot).astype(BF16) for x, hot in zip(tables, hots)])
        for i, n in enumerate(ns):
            eL[n, t] = out[0][i][:, 0:MARGIN]
            eR[n, t] = out[2][i][:, MARGIN:256]
        for i, n in enumerate(ns):
            own[n, :, 0:128] = out[0][i][:, MARGIN:256]
            own[n, :, 128:384] = out[1][i]
            own[n, :, 384:512] = out[2][i][:, 0:MARGIN]

    def send_halo(n, t):
        for copy in halo(n, t):
            copy.start()

    def wait_halo(n, t):
        for copy in halo(n, t):
            copy.wait_recv()

    def merge_with(n, t, d, e):
        lane = iota((1, 128), 1)
        front = jnp.where(
            lane < d, hL[n, t].astype(F32), own[n, :, 0:128].astype(F32)
        ).astype(BF16)
        back = jnp.where(
            lane + 384 >= e, hR[n, t].astype(F32), own[n, :, 384:512].astype(F32)
        ).astype(BF16)
        own[n, :, 0:128] = front
        own[n, :, 384:512] = back

    def merge(n, t):
        at = row_of(n, t)
        merge_with(n, t, dref[pl.ds(at, 1), :], eref[pl.ds(at, 1), :])

    def step(ns, t):
        lane = iota((1, 128), 1)
        halves = [slice(b * 256, (b + 1) * 256) for b in range(2)]
        xs = [[own[n, :, c] for c in halves] for n in ns]
        mats = [mT[n] for n in ns]
        noise_t = [nT[t, :, c].astype(F32) for c in halves]
        shocks = [vn[pl.ds(t, 1), c] for c in halves]
        y = yb[t]
        y = jnp.concatenate([y, y], axis=1)
        load = lT[...]
        clouds, hs = [], []
        for n, x, mat in zip(ns, xs, mats):
            a = anc_s[n]
            center, persist, spread = vm_s[a], vp_s[a], vs_s[a]
            cloud, level = [], []
            for b in range(2):
                vol = x[b][K:EXT].astype(F32)[0:1]
                h = center + persist * (vol - center) + spread * shocks[b]
                drift = nn(mat, x[b][0:K])
                cloud.append((drift + jnp.exp(0.5 * h) * noise_t[b]).astype(BF16))
                level.append(h)
            clouds.append(cloud)
            hs.append(level)
        tables = []
        for n, cloud, level in zip(ns, clouds, hs):
            h = jnp.concatenate(level, axis=1)
            cT[n, 0:K, 0:256] = cloud[0]
            cT[n, 0:K, 256:512] = cloud[1]
            o_vol[pl.ds(n, 1), :] = h.astype(BF16).astype(F32)
            wide = jnp.broadcast_to(h, (EXT - K, SD)).astype(BF16)
            tables.append(
                jnp.concatenate([jnp.concatenate(cloud, axis=1), wide], axis=0)
            )

        def weigh():
            for n, cloud in zip(ns, clouds):
                prec = op_s[anc_s[n]]
                parts = []
                for b in range(2):
                    miss = y - nn(load, cloud[b])
                    ssq = jnp.sum(miss * miss, axis=0, keepdims=True)
                    parts.append(-0.5 * prec * ssq)
                logw = jnp.concatenate(parts, axis=1)
                logw = logw + 0.5 * M * jnp.log(jnp.full((1, 1), prec, F32))
                peak = jnp.max(logw, axis=1, keepdims=True)
                mass = jnp.sum(jnp.exp(logw - peak), axis=1, keepdims=True)
                here = lane == t
                for at, value in ((n, peak), (PD + n, mass)):
                    old = stats[pl.ds(at, 1), :]
                    stats[pl.ds(at, 1), :] = jnp.where(here, value, old)

        return tables, weigh

    def finish(n):
        for b in range(2):
            block = cT[n, 0:K, b * 256 : (b + 1) * 256]
            osb[n, b * 256 : (b + 1) * 256, :] = nt(eyer[...], block).astype(BF16)
        pltpu.make_async_copy(osb.at[n], o_states.at[n], out_sem.at[n]).start()

    def ask():
        for side in range(2):
            n = LAST + side
            row = picks_of(n, 0)
            for b in range(FRAME // 128):
                req[side, b : b + 1, :] = row[:, b * 128 : (b + 1) * 128]
            req[side, 6:7, :] = dref[pl.ds(perm_s[n], 1), :]
            req[side, 7:8, :] = eref[pl.ds(perm_s[n], 1), :]
        for side in range(2):
            @pl.when(takes[side])
            def _(side=side):
                request(side).start()


    def take_request(d):
        @pl.when(gives[d])
        def _():
            request_any(d).wait_recv()

        at = STEPS * PD + d
        cz[pl.ds(at, 1), :] = jnp.concatenate(
            [reqin[d, b : b + 1, :] for b in range(FRAME // 128)], axis=1
        )
        dref[pl.ds(at, 1), :] = reqin[d, 6:7, :]
        eref[pl.ds(at, 1), :] = reqin[d, 7:8, :]

    def task(m, _):
        code = PACKED[0]
        for k in range(1, len(PACKED)):
            code = jnp.where(m // 4 == k, PACKED[k], code)
        code = lax.shift_right_logical(code, 7 * (m % 4)) & 127
        kind, r, t = code // 16, (code // 4) % 4, code % 4
        pair = (2 * r, 2 * r + 1)
        late = (r == KEEP - 1) & (t == 0)

        @pl.when(kind == BUILD)
        def _():
            for n in pair:
                pass_two(n)
            for n in pair:
                pass_on(n + 2)
            for n in pair:
                arrive(n)
            for n in pair:
                build(n)
            draw(pair, 0, [cT[n] for n in pair])
            for n in pair:
                send_halo(n, 0)

        @pl.when(kind == SERVE)
        def _():
            for d in range(2):
                take_request(d)
            for side in range(2):
                src = src_s[LAST + side]
                put_cloud(LAST + side, st[src], lvf[pl.ds(src, 1), :])
            draw((LAST, LAST + 1), 0, [cT[LAST], cT[LAST + 1]])
            send_halo(LAST, 0)
            send_halo(LAST + 1, 0)
            for d in range(2):
                put_cloud(PD + d, sc[LAST + d], sv[d, KEEP - 1 : KEEP, :])
            draw((PD, PD + 1), 0, [cT[PD], cT[PD + 1]])
            for d in range(2):
                send_halo(PD + d, 0)

        @pl.when(kind == PASS)
        def _():
            for d in range(2):
                wait_halo(PD + d, 0)
            for d in range(2):
                merge(PD + d, 0)
            for d in range(2):
                @pl.when(gives[d])
                def _(d=d):
                    send_drawn(d).start()

            for n in (LAST, LAST + 1):
                wait_halo(n, 0)
            for n in (LAST, LAST + 1):
                merge(n, 0)

        @pl.when((kind == GO) & late)
        def _():
            for side in range(2):
                @pl.when(takes[side])
                def _(side=side):
                    send_drawn(side).wait_recv()

            for side in range(2):
                n = LAST + side
                own[n] = jnp.where(
                    rem_s[n] == 1, rcT[side].astype(F32), own[n].astype(F32)
                ).astype(BF16)

        @pl.when(((kind == GO) | (kind == END)) & jnp.logical_not(late))
        def _():
            for n in pair:
                wait_halo(n, t)
            for n in pair:
                merge(n, t)

        @pl.when((kind == GO) & (t == 0))
        def _():
            for n in pair:
                build_mat(n)

        @pl.when((kind == GO) & (t == 0) & (r == KEEP - 2))
        def _():
            for n in (LAST, LAST + 1):
                pass_two(n)

        @pl.when(kind == GO)
        def _():
            tables, weigh = step(pair, t)
            draw(pair, t + 1, tables)
            for n in pair:
                send_halo(n, t + 1)
            weigh()

        @pl.when(kind == END)
        def _():
            step(pair, t)[1]()

        @pl.when((kind == END) & (r < 2))
        def _():
            for n in pair:
                finish(n)

        return 0

    each_in = ((g > 0, 0), (g < TN - 1, 1))
    for cond, d in each_in:
        @pl.when(cond)
        def _(d=d):
            send_vol(d).wait_recv()

    ask()
    pass_on(0)
    pass_on(1)
    lax.fori_loop(0, len(ORDER), task, 0)

    def join(buf, here):
        order = [buf[(here + 8 - k) % 8] for k in range(8)]
        peak = order[0][0:PD]
        for x in order[1:]:
            peak = jnp.maximum(peak, x[0:PD])
        mass = jnp.zeros((PD, 128), F32)
        for x in order:
            mass = mass + x[PD:] * jnp.exp(x[0:PD] - peak)
        return peak, mass

    s1[0] = stats[...]
    for o in range(1, WN):
        group1(o, stats, s1, 2).start()

    for n in range(LAST - 2, PD):
        finish(n)
    for o in range(1, WN):
        group1(o, stats, s1, 2).wait_recv()
    peak, mass = join(s1, w)
    s2[0, 0:PD, :] = peak
    s2[0, PD:, :] = mass
    for o in range(1, 8):
        group2(o, s2.at[0], s2, 3).start()
    for o in range(1, 8):
        group2(o, s2.at[0], s2, 3).wait_recv()
    peak, mass = join(s2, z)
    live = lane8 < STEPS
    part = peak + jnp.log(jnp.where(live, mass, 1.0)) - math.log(SD * JN)
    total = jnp.sum(jnp.where(live, part, 0.0), axis=1, keepdims=True)
    o_ll[...] = jnp.broadcast_to(total, (PD, 128))

    for o in range(1, WN):
        group1(o, ctile, g1, 0).wait_send()
        group2(o, c2tile, g2, 1).wait_send()
        group1(o, stats, s1, 2).wait_send()
        group2(o, s2.at[0], s2, 3).wait_send()
    each_dir(lambda d: send_vol(d).wait_send())

    for d in range(2):
        @pl.when(gives[d])
        def _(d=d):
            send_drawn(d).wait_send()

        @pl.when(takes[d])
        def _(d=d):
            request(d).wait_send()

        for copy in halo(PD + d, 0):
            copy.wait_send()

    def drain(n, _):
        @pl.when(has_out(n))
        def _():
            send_mat(n).wait_send()

        @pl.when(has_out(n) & (n < LAST))
        def _():
            send_copy(n).wait_send()

        @pl.when(has_in(n))
        def _():
            forward(n).wait_send()
            for o in range(1, Q):
                spread(n, o).wait_send()

        def drain_t(t, _):
            to_left, to_right = halo(n, t)
            to_left.wait_send()
            to_right.wait_send()
            return 0

        lax.fori_loop(0, STEPS, drain_t, 0)
        pltpu.make_async_copy(osb.at[n], o_states.at[n], out_sem.at[n]).wait()
        return 0

    lax.fori_loop(0, PD, drain, 0)


def reorder(anc, pos, pr_s, res, vol, ll, o_states, o_vol, o_ll, buf, rows, sem):
    g = lax.axis_index("theta")

    def take(i):
        return pltpu.make_async_copy(res.at[pos[i]], buf.at[i], sem.at[0, i])

    def give(i):
        return pltpu.make_async_copy(buf.at[i], o_states.at[i], sem.at[1, i])

    for i in range(PD):
        take(i).start()
    lane = iota((1, 128), 1)
    out = jnp.zeros((1, 128), F32)
    for i in range(PD):
        rows[i : i + 1, :] = vol[pl.ds(pos[i], 1), :]
        value = ll[pl.ds(pos[i], 1), :] + pr_s[anc[g * PD + i]]
        out = jnp.where(lane == i, value, out)
    o_vol[...] = rows[...].astype(BF16)
    o_ll[...] = out[:, 0:PD]
    for i in range(PD):
        take(i).wait()
        give(i).start()
    for i in range(PD):
        give(i).wait()


def local(
    states, log_vol, transition, loading, yields, state_noise, vol_noise,
    vol_mean, vol_persist, vol_scale, obs_prec, prior_loglik,
    ancestors, counts, local_anc,
):
    smem = pl.BlockSpec(memory_space=pltpu.SMEM)
    vmem = pl.BlockSpec(memory_space=pltpu.VMEM)
    hbm = pl.BlockSpec(memory_space=pl.ANY)
    dma = pltpu.SemaphoreType.DMA
    v, s = pltpu.VMEM, pltpu.SMEM
    res, vol, ll, pos = pl.pallas_call(
        kernel,
        out_shape=(
            jax.ShapeDtypeStruct((PD, SD, K), BF16),
            jax.ShapeDtypeStruct((PD, SD), F32),
            jax.ShapeDtypeStruct((PD, 128), F32),
            jax.ShapeDtypeStruct((PD,), I32),
        ),
        in_specs=[smem] * 6 + [vmem] * 6 + [hbm] * 3,
        out_specs=(hbm, vmem, vmem, smem),
        scratch_shapes=[
            v((PD, SD, K), BF16), v((PD, K, K), BF16), v((STEPS, SD, K), BF16),
            v((PD, SD, K), BF16), v((PD, ROWS, K), BF16), v((2, PD, SD), F32),
            v((PD, SD, K), BF16), v((PD, 2, Q, ROWS, K), BF16), v((2, PD, SD), F32),
            v((2, EXT, SD), BF16), v((2, 8, 128), I32), v((2, 8, 128), I32),
            v((PD + 2, EXT, SD), BF16), v((PD + 2, EXT, SD), BF16), v((PD, K, K), BF16),
            v((STEPS, K, SD), BF16), v((M, K), BF16), v((STEPS, M, M), F32),
            v((PD + 2, STEPS, EXT, MARGIN), BF16), v((PD + 2, STEPS, EXT, MARGIN), BF16),
            v((PD + 2, STEPS, EXT, MARGIN), BF16), v((PD + 2, STEPS, EXT, MARGIN), BF16),
            v((PD, 128), I32), v((PD, 128), I32),
            v((8, PD, 128), I32), v((8, PD, 128), I32),
            v((STEPS * PD + 8, 128), I32), v((STEPS * PD + 8, 128), I32),
            v((STEPS * PD + 8, FRAME), I32),
            v((2 * PD, 128), F32), v((8, 2 * PD, 128), F32), v((8, 2 * PD, 128), F32),
            v((PD, SD), F32), v((PD, SD, K), BF16), v((K, K), BF16), v((256, 256), BF16),
            s((PD,), I32), s((PD,), I32), s((PD,), I32), s((PD,), I32), s((PD,), I32),
            dma((3,)), dma((2, PD)), dma((2, PD)), dma((2,)), dma((2,)), dma((PD, Q)), dma((PD, Q)), dma((PD,)), dma((PD,)),
            dma((2,)), dma((2,)), dma((2, PD + 2, STEPS)), dma((2, PD + 2, STEPS)),
            dma((4, 8)), dma((4, 8)), dma((PD,)),
        ],
        compiler_params=pltpu.CompilerParams(
            collective_id=0, has_side_effects=True, vmem_limit_bytes=63 << 20
        ),
    )(
        ancestors, vol_mean, vol_persist, vol_scale, obs_prec, prior_loglik,
        counts.transpose(0, 2, 1), log_vol, loading, yields, vol_noise,
        local_anc.reshape(STEPS * PD, FRAME), states, transition, state_noise,
    )
    final, final_vol, loglik = pl.pallas_call(
        reorder,
        out_shape=(
            jax.ShapeDtypeStruct((PD, SD, K), BF16),
            jax.ShapeDtypeStruct((PD, SD), BF16),
            jax.ShapeDtypeStruct((1, PD), F32),
        ),
        in_specs=[smem] * 3 + [hbm, vmem, vmem],
        out_specs=(hbm, vmem, vmem),
        scratch_shapes=[v((PD, SD, K), BF16), v((PD, SD), F32), dma((2, PD))],
        compiler_params=pltpu.CompilerParams(vmem_limit_bytes=63 << 20),
    )(ancestors, pos, prior_loglik, res, vol, ll)
    return final, final_vol, loglik.reshape(PD)


def solution(mesh):
    placed = (
        P("theta", "state", None),
        P("theta", "state"),
        P("theta", None, None),
        P(),
        P(),
        P(None, "state", None),
        P(None, "state"),
        P(),
        P(),
        P(),
        P(),
        P(),
        P(),
        P(None, "theta", "state"),
        P(None, "theta", "state"),
    )
    return jax.shard_map(
        local,
        mesh=mesh,
        in_specs=placed,
        out_specs=(P("theta", "state", None), P("theta", "state"), P("theta")),
        check_vma=False,
    )
```

```python
import math

import jax
import jax.numpy as jnp
from jax import lax
from jax.experimental import pallas as pl
from jax.experimental.pallas import tpu as pltpu
from jax.sharding import PartitionSpec as P

K = 256
M = 128
PD = 8
SD = 512
STEPS = 3
MARGIN = 128
FRAME = SD + 2 * MARGIN
EXT = K + 16
HALF = K // 2
Q = 2
ROWS = HALF // Q
KEEP = 4
LAST = 2 * KEEP - 2
TN = 4
JN = 64
WN = 8
BUILD, GO, END, SERVE, PASS = range(5)
ORDER = (
    (BUILD, 0, 0), (GO, 0, 0), (BUILD, 1, 0), (SERVE, 0, 0), (GO, 0, 1), (GO, 1, 0), (PASS, 0, 0), (BUILD, 2, 0), (END, 0, 2), (GO, 1, 1), (GO, 2, 0), (GO, 3, 0), (END, 1, 2), (GO, 2, 1), (GO, 3, 1), (END, 2, 2), (END, 3, 2),
)
PACKED = [
    sum((16 * k + 4 * r + t) << (7 * i) for i, (k, r, t) in enumerate(ORDER[at : at + 4]))
    for at in range(0, len(ORDER), 4)
]
F32 = jnp.float32
BF16 = jnp.bfloat16
I32 = jnp.int32
MESH = pl.DeviceIdType.MESH


def nt(a, b):
    return lax.dot_general(a, b, (((1,), (1,)), ((), ())), preferred_element_type=F32)


def nn(a, b):
    return lax.dot_general(a, b, (((1,), (0,)), ((), ())), preferred_element_type=F32)


def iota(shape, dim):
    return lax.broadcasted_iota(I32, shape, dim)


def eye(n):
    return jnp.where(iota((n, n), 0) == iota((n, n), 1), 1.0, 0.0).astype(BF16)


def kernel(
    anc, vm_s, vp_s, vs_s, op_s, pr_s,
    cnt, lv, ld, yl, vn, la, states, trans, noise,
    o_states, o_vol, o_ll, o_pos,
    st, tr, nz, sc, sm, sv, rc, rm, rv, rcT, req, reqin,
    cT, own, mT, nT, lT, yb, eL, eR, hL, hR,
    ctile, c2tile, g1, g2, dref, eref, cz, stats, s1, s2, lvf, osb, eyer, lines,
    perm_s, src_s, rem_s, anc_s, snd_s,
    ld_sem, th_ss, th_rs, rq_ss, rq_rs, zf_ss, zf_rs, fw_ss, fw_rs, tv_ss, tv_rs, hl_ss, hl_rs, g_ss, g_rs, out_sem,
):
    g = lax.axis_index("theta")
    j = lax.axis_index("state")
    z, w, core = j // WN, j % WN, j % 2
    zq = z % Q
    left, right = (j + JN - 1) % JN, (j + 1) % JN

    def dev(theta, state):
        return {"theta": theta, "state": state}

    barrier = pltpu.get_barrier_semaphore()

    def greet(theta, state):
        pl.semaphore_signal(
            barrier, inc=1, device_id=dev(theta, state), device_id_type=MESH
        )

    for o in range(1, 8):
        greet(g, ((z + o) % 8) * WN + w)
    for o in range(1, WN):
        greet(g, z * WN + (w + o) % WN)
    greet(g, left)
    greet(g, right)

    @pl.when(g > 0)
    def _():
        greet(g - 1, j)

    @pl.when(g < TN - 1)
    def _():
        greet(g + 1, j)

    load_st = pltpu.make_async_copy(states, st, ld_sem.at[0])
    load_tr = pltpu.make_async_copy(trans, tr, ld_sem.at[1])
    load_nz = pltpu.make_async_copy(noise, nz, ld_sem.at[2])
    load_st.start()
    load_tr.start()
    load_nz.start()

    a8 = [anc[g * PD + i] for i in range(PD)]
    off = [lax.shift_right_arithmetic(a, 3) - g for a in a8]
    below = [jnp.where(o == -1, 1, 0) for o in off]
    above = [jnp.where(o == 1, 1, 0) for o in off]
    nb, na, nl = 0, 0, 0
    rank_b, rank_a, rank_l = [], [], []
    for i in range(PD):
        rank_b.append(nb)
        rank_a.append(na)
        rank_l.append(nl)
        nb = nb + below[i]
        na = na + above[i]
        nl = nl + 1 - below[i] - above[i]
    free_b = KEEP - nb
    pos = []
    for i in range(PD):
        l = rank_l[i]
        home = jnp.where(l < free_b, 2 * (nb + l), 2 * (na + l - free_b) + 1)
        slot = jnp.where(
            below[i] == 1,
            2 * rank_b[i],
            jnp.where(above[i] == 1, 2 * rank_a[i] + 1, home),
        )
        pos.append(jnp.clip(slot, 0, PD - 1))
        o_pos[i] = pos[i]
    for n in range(PD):
        who, a = 0, 0
        for i in range(PD):
            hit = pos[i] == n
            who = jnp.where(hit, i, who)
            a = jnp.where(hit, a8[i], a)
        perm_s[n] = who
        anc_s[n] = a
        src_s[n] = a & (PD - 1)
        rem_s[n] = jnp.where(lax.shift_right_arithmetic(a, 3) == g, 0, 1)
    for d, peer in ((0, jnp.minimum(g + 1, TN - 1)), (1, jnp.maximum(g - 1, 0))):
        rank = 0
        chosen = [0] * KEEP
        for i in range(PD):
            a = anc[peer * PD + i]
            hit = jnp.where(lax.shift_right_arithmetic(a, 3) == g, 1, 0)
            for k in range(KEEP):
                take = jnp.where(rank == k, hit, 0)
                chosen[k] = jnp.where(take == 1, a & (PD - 1), chosen[k])
            rank = rank + hit
        for k in range(KEEP):
            snd_s[2 * k + d] = chosen[k]

    lane8 = iota((PD, 128), 1)
    tile = jnp.zeros((PD, 128), I32)
    for t in range(STEPS):
        line = jnp.broadcast_to(cnt[t].astype(F32), (PD, PD))
        line = jnp.where(iota((PD, PD), 0) == iota((PD, PD), 1), line, 0.0)
        column = jnp.sum(line, axis=1, keepdims=True).astype(I32)
        tile = jnp.where(lane8 == t, jnp.broadcast_to(column, (PD, 128)), tile)
    ctile[...] = tile
    lvf[...] = lv[...].astype(F32)
    for d in range(2):
        for k in range(KEEP):
            row = lvf[pl.ds(snd_s[2 * k + d], 1), :]
            sv[d, k : k + 1, :] = row
            sv[d, KEEP + k : KEEP + k + 1, :] = row
    load_st.wait()
    load_tr.wait()

    def fill(n, _):
        s = snd_s[n]
        sc[n] = st[s]
        sm[n] = tr[s, pl.ds(pl.multiple_of(core * HALF + zq * ROWS, ROWS), ROWS), :]
        return 0

    def send_copy(n):
        peer = jnp.where(n % 2 == 0, g + 1, g - 1)
        return pltpu.make_async_remote_copy(
            sc.at[n], rc.at[n], th_ss.at[0, n], th_rs.at[0, n],
            device_id=dev(peer, j), device_id_type=MESH,
        )

    def send_mat(n):
        peer = jnp.where(n % 2 == 0, g + 1, g - 1)
        return pltpu.make_async_remote_copy(
            sm.at[n], rm.at[n, core, zq], th_ss.at[1, n], th_rs.at[1, n],
            device_id=dev(peer, j), device_id_type=MESH,
        )

    def forward(n):
        return pltpu.make_async_remote_copy(
            rm.at[n, core], rm.at[n, core], fw_ss.at[n], fw_rs.at[n],
            device_id=dev(g, j + 1 - 2 * core), device_id_type=MESH,
        )

    def spread(n, o):
        return pltpu.make_async_remote_copy(
            rm.at[n, core, zq], rm.at[n, core, zq], zf_ss.at[n, o], zf_rs.at[n, o],
            device_id=dev(g, (z - zq + (zq + o) % Q) * WN + w), device_id_type=MESH,
        )

    def pass_on(n):
        @pl.when(has_in(n))
        def _():
            send_mat(n).wait_recv()
            for o in range(1, Q):
                spread(n, o).start()

    def pass_two(n):
        @pl.when(has_in(n))
        def _():
            for o in range(1, Q):
                came = rm.at[n, core, (zq + Q - o) % Q]
                pltpu.make_async_remote_copy(
                    came, came, zf_ss.at[n, o], zf_rs.at[n, o],
                    device_id=dev(g, (z - zq + (zq + o) % Q) * WN + w),
                    device_id_type=MESH,
                ).wait_recv()
            forward(n).start()

    def send_vol(d):
        peer = jnp.where(d == 0, g + 1, g - 1)
        return pltpu.make_async_remote_copy(
            sv.at[d], rv.at[d], tv_ss.at[d], tv_rs.at[d],
            device_id=dev(peer, j), device_id_type=MESH,
        )

    def group1(o, src, dst, u):
        return pltpu.make_async_remote_copy(
            src, dst.at[o], g_ss.at[u, o], g_rs.at[u, o],
            device_id=dev(g, z * WN + (w + o) % WN), device_id_type=MESH,
        )

    def group2(o, src, dst, u):
        return pltpu.make_async_remote_copy(
            src, dst.at[o], g_ss.at[u, o], g_rs.at[u, o],
            device_id=dev(g, ((z + o) % 8) * WN + w), device_id_type=MESH,
        )

    lax.fori_loop(0, 4, fill, 0)
    pl.semaphore_wait(
        barrier, 16 + jnp.where(g > 0, 1, 0) + jnp.where(g < TN - 1, 1, 0)
    )
    for o in range(1, WN):
        group1(o, ctile, g1, 0).start()

    def each_dir(fn):
        @pl.when(g < TN - 1)
        def _():
            fn(0)

        @pl.when(g > 0)
        def _():
            fn(1)

    def has_in(n):
        return jnp.where(n % 2 == 0, g > 0, g < TN - 1)

    def has_out(n):
        return jnp.where(n % 2 == 0, g < TN - 1, g > 0)

    each_dir(lambda d: send_vol(d).start())

    def start_mat(n, _):
        @pl.when(has_out(n))
        def _():
            send_mat(n).start()

        return 0

    def start_copy(n, _):
        @pl.when(has_out(n))
        def _():
            send_copy(n).start()

        return 0

    lax.fori_loop(0, 2, start_copy, 0)
    lax.fori_loop(0, 4, start_mat, 0)
    lax.fori_loop(4, 2 * KEEP, fill, 0)

    def start_more(r, _):
        for d in range(2):
            start_mat(2 * r + 2 + d, 0)
        for d in range(2):
            start_copy(2 * r + d, 0)
        return 0

    lax.fori_loop(1, KEEP - 1, start_more, 0)

    def request(side):
        return pltpu.make_async_remote_copy(
            req.at[side], reqin.at[side], rq_ss.at[side], rq_rs.at[side],
            device_id=dev(g - 1 if side == 0 else g + 1, j), device_id_type=MESH,
        )

    def request_any(d):
        return pltpu.make_async_remote_copy(
            req.at[d], reqin.at[d], rq_ss.at[d], rq_rs.at[d],
            device_id=dev(jnp.where(d == 0, g - 1, g + 1), j), device_id_type=MESH,
        )

    def send_drawn(d):
        return pltpu.make_async_remote_copy(
            own.at[PD + d], rcT.at[d], th_ss.at[0, LAST + d], th_rs.at[0, LAST + d],
            device_id=dev(jnp.where(d == 0, g + 1, g - 1), j), device_id_type=MESH,
        )

    takes = (g > 0, g < TN - 1)
    gives = (g < TN - 1, g > 0)

    eyer[...] = eye(K)
    lines[...] = iota((256, 256), 0).astype(F32).astype(BF16)
    load_nz.wait()
    for t in range(STEPS):
        nT[t] = nt(eyer[...], nz[t]).astype(BF16)
        yb[t] = jnp.transpose(jnp.broadcast_to(yl[t : t + 1, :], (M, M)))
    lT[...] = nt(eye(M), ld[...]).astype(BF16)
    stats[...] = jnp.zeros_like(stats)

    before = jnp.zeros((PD, 128), I32)
    whole = ctile[...]
    for o in range(1, WN):
        group1(o, ctile, g1, 0).wait_recv()
        got = g1[o]
        source = (w + WN - o) % WN
        before = before + jnp.where(source < w, got, 0)
        whole = whole + got
    c2tile[...] = whole
    for o in range(1, 8):
        group2(o, c2tile, g2, 1).start()
    for o in range(1, 8):
        group2(o, c2tile, g2, 1).wait_recv()
        source = (z + 8 - o) % 8
        before = before + jnp.where(source < z, g2[o], 0)
    first = before - SD * j
    for t in range(STEPS):
        d = jnp.broadcast_to(first[:, t : t + 1], (PD, 128))
        e = d + jnp.broadcast_to(tile[:, t : t + 1], (PD, 128))
        dref[t * PD : (t + 1) * PD, :] = d
        eref[t * PD : (t + 1) * PD, :] = e
        shift = jnp.concatenate([d + MARGIN] * (FRAME // 128), axis=1)
        x = la[t * PD : (t + 1) * PD, :]
        for b in range(9):
            x = jnp.where((shift & (1 << b)) != 0, pltpu.roll(x, 1 << b, 1), x)
        cz[t * PD : (t + 1) * PD, :] = x

    def halo(n, t):
        to_left = pltpu.make_async_remote_copy(
            eL.at[n, t], hR.at[n, t], hl_ss.at[0, n, t], hl_rs.at[0, n, t],
            device_id=dev(g, left), device_id_type=MESH,
        )
        to_right = pltpu.make_async_remote_copy(
            eR.at[n, t], hL.at[n, t], hl_ss.at[1, n, t], hl_rs.at[1, n, t],
            device_id=dev(g, right), device_id_type=MESH,
        )
        return to_left, to_right

    def arrive(n):
        @pl.when(has_in(n))
        def _():
            send_copy(n).wait_recv()


    def put_cloud(n, cloud, vol):
        cT[n, 0:K, :] = nt(eyer[...], cloud).astype(BF16)
        cT[n, K:EXT, :] = jnp.broadcast_to(vol, (EXT - K, SD)).astype(BF16)

    def build_mat(n):
        @pl.when(has_in(n))
        def _():
            forward(n).wait_recv()

        pieces = [rm[n, c, q] for c in range(2) for q in range(Q)]
        got = jnp.concatenate(pieces, axis=0).astype(F32)
        mat = jnp.where(rem_s[n] == 1, got, tr[src_s[n]].astype(F32)).astype(BF16)
        mT[n] = nt(eyer[...], mat).astype(BF16)

    def build(n):
        src = src_s[n]
        remote = rem_s[n] == 1
        cloud = jnp.where(remote, rc[n].astype(F32), st[src].astype(F32)).astype(BF16)
        got = rv[n % 2, pl.ds(n // 2, 1), :]
        put_cloud(n, cloud, jnp.where(remote, got, lvf[pl.ds(src, 1), :]))

    def row_of(n, t):
        return jnp.where(n < PD, t * PD + perm_s[jnp.minimum(n, PD - 1)], STEPS * PD + n - PD)

    def picks_of(n, t):
        return cz[pl.ds(row_of(n, t), 1), :]

    def draw(ns, t, tables):
        rows = lines[...]
        picks = [picks_of(n, t).astype(F32) for n in ns]
        out = []
        for b in range(FRAME // 256):
            hots = []
            for pick in picks:
                row = pick[:, b * 256 : (b + 1) * 256]
                hots.append(
                    jnp.concatenate(
                        [
                            jnp.where(
                                rows == (row - float(part * 256)).astype(BF16),
                                jnp.ones((), BF16),
                                jnp.zeros((), BF16),
                            )
                            for part in range(2)
                        ],
                        axis=0,
                    )
                )
            out.append([nn(x, hot).astype(BF16) for x, hot in zip(tables, hots)])
        for i, n in enumerate(ns):
            eL[n, t] = out[0][i][:, 0:MARGIN]
            eR[n, t] = out[2][i][:, MARGIN:256]
        for i, n in enumerate(ns):
            own[n, :, 0:128] = out[0][i][:, MARGIN:256]
            own[n, :, 128:384] = out[1][i]
            own[n, :, 384:512] = out[2][i][:, 0:MARGIN]

    def send_halo(n, t):
        for copy in halo(n, t):
            copy.start()

    def wait_halo(n, t):
        for copy in halo(n, t):
            copy.wait_recv()

    def merge_with(n, t, d, e):
        lane = iota((1, 128), 1)
        front = jnp.where(
            lane < d, hL[n, t].astype(F32), own[n, :, 0:128].astype(F32)
        ).astype(BF16)
        back = jnp.where(
            lane + 384 >= e, hR[n, t].astype(F32), own[n, :, 384:512].astype(F32)
        ).astype(BF16)
        own[n, :, 0:128] = front
        own[n, :, 384:512] = back

    def merge(n, t):
        at = row_of(n, t)
        merge_with(n, t, dref[pl.ds(at, 1), :], eref[pl.ds(at, 1), :])

    def step(ns, t):
        lane = iota((1, 128), 1)
        halves = [slice(b * 256, (b + 1) * 256) for b in range(2)]
        xs = [[own[n, :, c] for c in halves] for n in ns]
        mats = [mT[n] for n in ns]
        noise_t = [nT[t, :, c].astype(F32) for c in halves]
        shocks = [vn[pl.ds(t, 1), c] for c in halves]
        y = yb[t]
        y = jnp.concatenate([y, y], axis=1)
        load = lT[...]
        clouds, hs = [], []
        for n, x, mat in zip(ns, xs, mats):
            a = anc_s[n]
            center, persist, spread = vm_s[a], vp_s[a], vs_s[a]
            cloud, level = [], []
            for b in range(2):
                vol = x[b][K:EXT].astype(F32)[0:1]
                h = center + persist * (vol - center) + spread * shocks[b]
                drift = nn(mat, x[b][0:K])
                cloud.append((drift + jnp.exp(0.5 * h) * noise_t[b]).astype(BF16))
                level.append(h)
            clouds.append(cloud)
            hs.append(level)
        tables = []
        for n, cloud, level in zip(ns, clouds, hs):
            h = jnp.concatenate(level, axis=1)
            cT[n, 0:K, 0:256] = cloud[0]
            cT[n, 0:K, 256:512] = cloud[1]
            o_vol[pl.ds(n, 1), :] = h.astype(BF16).astype(F32)
            wide = jnp.broadcast_to(h, (EXT - K, SD)).astype(BF16)
            tables.append(
                jnp.concatenate([jnp.concatenate(cloud, axis=1), wide], axis=0)
            )

        def weigh():
            for n, cloud in zip(ns, clouds):
                prec = op_s[anc_s[n]]
                parts = []
                for b in range(2):
                    miss = y - nn(load, cloud[b])
                    ssq = jnp.sum(miss * miss, axis=0, keepdims=True)
                    parts.append(-0.5 * prec * ssq)
                logw = jnp.concatenate(parts, axis=1)
                logw = logw + 0.5 * M * jnp.log(jnp.full((1, 1), prec, F32))
                peak = jnp.max(logw, axis=1, keepdims=True)
                mass = jnp.sum(jnp.exp(logw - peak), axis=1, keepdims=True)
                here = lane == t
                for at, value in ((n, peak), (PD + n, mass)):
                    old = stats[pl.ds(at, 1), :]
                    stats[pl.ds(at, 1), :] = jnp.where(here, value, old)

        return tables, weigh

    def finish(n):
        for b in range(2):
            block = cT[n, 0:K, b * 256 : (b + 1) * 256]
            osb[n, b * 256 : (b + 1) * 256, :] = nt(eyer[...], block).astype(BF16)
        pltpu.make_async_copy(osb.at[n], o_states.at[n], out_sem.at[n]).start()

    def ask():
        for side in range(2):
            n = LAST + side
            row = picks_of(n, 0)
            for b in range(FRAME // 128):
                req[side, b : b + 1, :] = row[:, b * 128 : (b + 1) * 128]
            req[side, 6:7, :] = dref[pl.ds(perm_s[n], 1), :]
            req[side, 7:8, :] = eref[pl.ds(perm_s[n], 1), :]
        for side in range(2):
            @pl.when(takes[side])
            def _(side=side):
                request(side).start()


    def take_request(d):
        @pl.when(gives[d])
        def _():
            request_any(d).wait_recv()

        at = STEPS * PD + d
        cz[pl.ds(at, 1), :] = jnp.concatenate(
            [reqin[d, b : b + 1, :] for b in range(FRAME // 128)], axis=1
        )
        dref[pl.ds(at, 1), :] = reqin[d, 6:7, :]
        eref[pl.ds(at, 1), :] = reqin[d, 7:8, :]

    def task(m, _):
        code = PACKED[0]
        for k in range(1, len(PACKED)):
            code = jnp.where(m // 4 == k, PACKED[k], code)
        code = lax.shift_right_logical(code, 7 * (m % 4)) & 127
        kind, r, t = code // 16, (code // 4) % 4, code % 4
        pair = (2 * r, 2 * r + 1)
        late = (r == KEEP - 1) & (t == 0)

        @pl.when(kind == BUILD)
        def _():
            for n in pair:
                arrive(n)
            for n in pair:
                build(n)
            draw(pair, 0, [cT[n] for n in pair])
            for n in pair:
                send_halo(n, 0)

            @pl.when(r == 0)
            def _():
                for n in pair:
                    pass_on(n)

            for n in pair:
                pass_two(n)
            for n in pair:
                pass_on(n + 2)

        @pl.when(kind == SERVE)
        def _():
            for d in range(2):
                take_request(d)
            for side in range(2):
                src = src_s[LAST + side]
                put_cloud(LAST + side, st[src], lvf[pl.ds(src, 1), :])
            draw((LAST, LAST + 1), 0, [cT[LAST], cT[LAST + 1]])
            send_halo(LAST, 0)
            send_halo(LAST + 1, 0)
            for d in range(2):
                put_cloud(PD + d, sc[LAST + d], sv[d, KEEP - 1 : KEEP, :])
            draw((PD, PD + 1), 0, [cT[PD], cT[PD + 1]])
            for d in range(2):
                send_halo(PD + d, 0)

        @pl.when(kind == PASS)
        def _():
            for d in range(2):
                wait_halo(PD + d, 0)
            for d in range(2):
                merge(PD + d, 0)
            for d in range(2):
                @pl.when(gives[d])
                def _(d=d):
                    send_drawn(d).start()

            for n in (LAST, LAST + 1):
                wait_halo(n, 0)
            for n in (LAST, LAST + 1):
                merge(n, 0)

        @pl.when((kind == GO) & late)
        def _():
            for side in range(2):
                @pl.when(takes[side])
                def _(side=side):
                    send_drawn(side).wait_recv()

            for side in range(2):
                n = LAST + side
                own[n] = jnp.where(
                    rem_s[n] == 1, rcT[side].astype(F32), own[n].astype(F32)
                ).astype(BF16)

        @pl.when(((kind == GO) | (kind == END)) & jnp.logical_not(late))
        def _():
            for n in pair:
                wait_halo(n, t)
            for n in pair:
                merge(n, t)

        @pl.when((kind == GO) & (t == 0))
        def _():
            for n in pair:
                build_mat(n)

        @pl.when((kind == GO) & (t == 0) & (r == KEEP - 2))
        def _():
            for n in (LAST, LAST + 1):
                pass_two(n)

        @pl.when(kind == GO)
        def _():
            tables, weigh = step(pair, t)
            draw(pair, t + 1, tables)
            for n in pair:
                send_halo(n, t + 1)
            weigh()

        @pl.when(kind == END)
        def _():
            step(pair, t)[1]()

        @pl.when((kind == END) & (r < 2))
        def _():
            for n in pair:
                finish(n)

        return 0

    each_in = ((g > 0, 0), (g < TN - 1, 1))
    for cond, d in each_in:
        @pl.when(cond)
        def _(d=d):
            send_vol(d).wait_recv()

    ask()
    lax.fori_loop(0, len(ORDER), task, 0)

    def join(buf, here):
        order = [buf[(here + 8 - k) % 8] for k in range(8)]
        peak = order[0][0:PD]
        for x in order[1:]:
            peak = jnp.maximum(peak, x[0:PD])
        mass = jnp.zeros((PD, 128), F32)
        for x in order:
            mass = mass + x[PD:] * jnp.exp(x[0:PD] - peak)
        return peak, mass

    s1[0] = stats[...]
    for o in range(1, WN):
        group1(o, stats, s1, 2).start()

    for n in range(LAST - 2, PD):
        finish(n)
    for o in range(1, WN):
        group1(o, stats, s1, 2).wait_recv()
    peak, mass = join(s1, w)
    s2[0, 0:PD, :] = peak
    s2[0, PD:, :] = mass
    for o in range(1, 8):
        group2(o, s2.at[0], s2, 3).start()
    for o in range(1, 8):
        group2(o, s2.at[0], s2, 3).wait_recv()
    peak, mass = join(s2, z)
    live = lane8 < STEPS
    part = peak + jnp.log(jnp.where(live, mass, 1.0)) - math.log(SD * JN)
    total = jnp.sum(jnp.where(live, part, 0.0), axis=1, keepdims=True)
    o_ll[...] = jnp.broadcast_to(total, (PD, 128))

    for o in range(1, WN):
        group1(o, ctile, g1, 0).wait_send()
        group2(o, c2tile, g2, 1).wait_send()
        group1(o, stats, s1, 2).wait_send()
        group2(o, s2.at[0], s2, 3).wait_send()
    each_dir(lambda d: send_vol(d).wait_send())

    for d in range(2):
        @pl.when(gives[d])
        def _(d=d):
            send_drawn(d).wait_send()

        @pl.when(takes[d])
        def _(d=d):
            request(d).wait_send()

        for copy in halo(PD + d, 0):
            copy.wait_send()

    def drain(n, _):
        @pl.when(has_out(n))
        def _():
            send_mat(n).wait_send()

        @pl.when(has_out(n) & (n < LAST))
        def _():
            send_copy(n).wait_send()

        @pl.when(has_in(n))
        def _():
            forward(n).wait_send()
            for o in range(1, Q):
                spread(n, o).wait_send()

        def drain_t(t, _):
            to_left, to_right = halo(n, t)
            to_left.wait_send()
            to_right.wait_send()
            return 0

        lax.fori_loop(0, STEPS, drain_t, 0)
        pltpu.make_async_copy(osb.at[n], o_states.at[n], out_sem.at[n]).wait()
        return 0

    lax.fori_loop(0, PD, drain, 0)


def reorder(anc, pos, pr_s, res, vol, ll, o_states, o_vol, o_ll, buf, rows, sem):
    g = lax.axis_index("theta")

    def take(i):
        return pltpu.make_async_copy(res.at[pos[i]], buf.at[i], sem.at[0, i])

    def give(i):
        return pltpu.make_async_copy(buf.at[i], o_states.at[i], sem.at[1, i])

    for i in range(PD):
        take(i).start()
    lane = iota((1, 128), 1)
    out = jnp.zeros((1, 128), F32)
    for i in range(PD):
        rows[i : i + 1, :] = vol[pl.ds(pos[i], 1), :]
        value = ll[pl.ds(pos[i], 1), :] + pr_s[anc[g * PD + i]]
        out = jnp.where(lane == i, value, out)
    o_vol[...] = rows[...].astype(BF16)
    o_ll[...] = out[:, 0:PD]
    for i in range(PD):
        take(i).wait()
        give(i).start()
    for i in range(PD):
        give(i).wait()


def local(
    states, log_vol, transition, loading, yields, state_noise, vol_noise,
    vol_mean, vol_persist, vol_scale, obs_prec, prior_loglik,
    ancestors, counts, local_anc,
):
    smem = pl.BlockSpec(memory_space=pltpu.SMEM)
    vmem = pl.BlockSpec(memory_space=pltpu.VMEM)
    hbm = pl.BlockSpec(memory_space=pl.ANY)
    dma = pltpu.SemaphoreType.DMA
    v, s = pltpu.VMEM, pltpu.SMEM
    res, vol, ll, pos = pl.pallas_call(
        kernel,
        out_shape=(
            jax.ShapeDtypeStruct((PD, SD, K), BF16),
            jax.ShapeDtypeStruct((PD, SD), F32),
            jax.ShapeDtypeStruct((PD, 128), F32),
            jax.ShapeDtypeStruct((PD,), I32),
        ),
        in_specs=[smem] * 6 + [vmem] * 6 + [hbm] * 3,
        out_specs=(hbm, vmem, vmem, smem),
        scratch_shapes=[
            v((PD, SD, K), BF16), v((PD, K, K), BF16), v((STEPS, SD, K), BF16),
            v((PD, SD, K), BF16), v((PD, ROWS, K), BF16), v((2, PD, SD), F32),
            v((PD, SD, K), BF16), v((PD, 2, Q, ROWS, K), BF16), v((2, PD, SD), F32),
            v((2, EXT, SD), BF16), v((2, 8, 128), I32), v((2, 8, 128), I32),
            v((PD + 2, EXT, SD), BF16), v((PD + 2, EXT, SD), BF16), v((PD, K, K), BF16),
            v((STEPS, K, SD), BF16), v((M, K), BF16), v((STEPS, M, M), F32),
            v((PD + 2, STEPS, EXT, MARGIN), BF16), v((PD + 2, STEPS, EXT, MARGIN), BF16),
            v((PD + 2, STEPS, EXT, MARGIN), BF16), v((PD + 2, STEPS, EXT, MARGIN), BF16),
            v((PD, 128), I32), v((PD, 128), I32),
            v((8, PD, 128), I32), v((8, PD, 128), I32),
            v((STEPS * PD + 8, 128), I32), v((STEPS * PD + 8, 128), I32),
            v((STEPS * PD + 8, FRAME), I32),
            v((2 * PD, 128), F32), v((8, 2 * PD, 128), F32), v((8, 2 * PD, 128), F32),
            v((PD, SD), F32), v((PD, SD, K), BF16), v((K, K), BF16), v((256, 256), BF16),
            s((PD,), I32), s((PD,), I32), s((PD,), I32), s((PD,), I32), s((PD,), I32),
            dma((3,)), dma((2, PD)), dma((2, PD)), dma((2,)), dma((2,)), dma((PD, Q)), dma((PD, Q)), dma((PD,)), dma((PD,)),
            dma((2,)), dma((2,)), dma((2, PD + 2, STEPS)), dma((2, PD + 2, STEPS)),
            dma((4, 8)), dma((4, 8)), dma((PD,)),
        ],
        compiler_params=pltpu.CompilerParams(
            collective_id=0, has_side_effects=True, vmem_limit_bytes=63 << 20
        ),
    )(
        ancestors, vol_mean, vol_persist, vol_scale, obs_prec, prior_loglik,
        counts.transpose(0, 2, 1), log_vol, loading, yields, vol_noise,
        local_anc.reshape(STEPS * PD, FRAME), states, transition, state_noise,
    )
    final, final_vol, loglik = pl.pallas_call(
        reorder,
        out_shape=(
            jax.ShapeDtypeStruct((PD, SD, K), BF16),
            jax.ShapeDtypeStruct((PD, SD), BF16),
            jax.ShapeDtypeStruct((1, PD), F32),
        ),
        in_specs=[smem] * 3 + [hbm, vmem, vmem],
        out_specs=(hbm, vmem, vmem),
        scratch_shapes=[v((PD, SD, K), BF16), v((PD, SD), F32), dma((2, PD))],
        compiler_params=pltpu.CompilerParams(vmem_limit_bytes=63 << 20),
    )(ancestors, pos, prior_loglik, res, vol, ll)
    return final, final_vol, loglik.reshape(PD)


def solution(mesh):
    placed = (
        P("theta", "state", None),
        P("theta", "state"),
        P("theta", None, None),
        P(),
        P(),
        P(None, "state", None),
        P(None, "state"),
        P(),
        P(),
        P(),
        P(),
        P(),
        P(),
        P(None, "theta", "state"),
        P(None, "theta", "state"),
    )
    return jax.shard_map(
        local,
        mesh=mesh,
        in_specs=placed,
        out_specs=(P("theta", "state", None), P("theta", "state"), P("theta")),
        check_vma=False,
    )
```
